256 devices in a mesh: firm: 16 (over y_lo, z), tm: 16 (over x, y_hi, core).
Axes of the slice: x: 4, y: 4 (y_hi: 2, y_lo: 2; y = y_hi * 2 + y_lo), z: 8, core: 2. Of those that a mesh axis runs over, the one named last changes fastest.
Arguments:
- features: bfloat16 [8192, 32, 128], P('firm', 'tm'), may hold values from -6 to 6
- cotangent: bfloat16 [8192, 32, 128], P('firm', 'tm'), may hold values from -6 to 6
- tiles: bfloat16 [64, 64, 128, 128], P('firm'), may hold values from -0.125 to 0.125
- mask: int32 [64, 64], P('firm'), may hold values 0 or 1
- w_prev: bfloat16 [2, 128, 256], replicated, may hold values from -0.375 to 0.375
- w_cur: bfloat16 [2, 128, 256], replicated, may hold values from -0.375 to 0.375
- w_self: bfloat16 [2, 128, 128], replicated, may hold values from -0.5 to 0.5
- w_nbr: bfloat16 [2, 128, 128], replicated, may hold values from -0.5 to 0.5
- dilations: int32 [2], replicated, may hold values from 1 to 2, as said below
Outputs:
- grad_features: float32 [8192, 32, 128], P('firm', 'tm')
- grad_prev: float32 [2, 128, 256], replicated
- grad_cur: float32 [2, 128, 256], replicated
- grad_self: float32 [2, 128, 128], replicated
- grad_nbr: float32 [2, 128, 128], replicated
The draws below stay inside these ranges and needn't reach their ends.
Inputs may be any that keep to these rules, and one draw needn't show every extreme that they name: `dilations`: each layer's dilation lies between 1 and 2; some layer has dilation 1 and some layer has dilation 2.
All inputs are finite; a program needn't handle non-finite values. No bound on the sum of `mask` on one device may be relied on, other than what follows from the above.
Results may differ from the reference program's by a relative error of at most 0.007.
Values may be sent and summed in bfloat16 or wider, within the bound.
No kernel may reach another device: no remote copies, remote signals or barrier semaphores. Data moves between devices by JAX's collectives and lax.ppermute only.
A program may use at most 128 MiB of HBM per device.

```python
import jax
import jax.numpy as jnp
from jax import lax

DD = 2
BS = 128
C = 128
L = 2
NB = 64
NF = 8192
DAYS = 32


def draw_dilations(key, part):
    base = jax.random.randint(jax.random.fold_in(key, 11), (L,), 1, DD + 1)
    chosen = jax.random.randint(jax.random.fold_in(key, 12), (), 0, L)
    second = (chosen + 1) % L
    layer_ids = jnp.arange(L)
    base = jnp.where(layer_ids == second, 1, base)
    return jnp.where(layer_ids == chosen, DD, base).astype(jnp.int32)


def set_ends(result, stream_key, least, top_value):
    index_at = [jax.random.randint(jax.random.fold_in(stream_key, axis), (), 0, length) for axis, length in enumerate(result.shape)]
    main_axis = result.shape.index(max(result.shape))
    beside = index_at[:main_axis] + [(index_at[main_axis] + 1) % result.shape[main_axis]] + index_at[main_axis + 1:]
    return result.at[tuple(index_at)].set(least).at[tuple(beside)].set(top_value)


def steps_of(own_key, extent, split, smallest, largest):
    def one(position, shards_of):
        draws = jax.random.uniform(jax.random.fold_in(jax.random.fold_in(own_key, 6), position), (shards_of,), jnp.float32, smallest / len(split), largest / len(split))
        return jnp.repeat(jnp.exp(draws), extent[position] // shards_of).reshape((-1,) + (1,) * (len(extent) - position - 1))

    gain = one(*split[0])
    for cut in split[1:]:
        gain = gain * one(*cut)
    return gain


def normal_values(rng, dims, width, limit, pieces=(), kind=jnp.bfloat16):
    loudness = steps_of(rng, dims, pieces, -0.22, 0.18) if pieces else 1.0
    array = jax.random.normal(rng, dims, jnp.float32) * width * loudness
    return jnp.minimum(jnp.maximum(array, -limit), limit).astype(kind)


def setup_inputs(seed: int = 0) -> dict:
    streams_of = jax.random.split(jax.random.key(seed), 10)
    features = normal_values(streams_of[0], (NF, DAYS, C), 1.0, 6.0, ((0, 16), (1, 16)))
    cotangent = normal_values(streams_of[1], (NF, DAYS, C), 1.0, 6.0, ((0, 16), (1, 16)))
    tiles = normal_values(streams_of[2], (NB, NB, BS, BS), (NB * BS // 4) ** -0.5, 0.125, ((0, 16),))
    mask = set_ends((jax.random.randint(streams_of[3], (NB, NB), 0, 4) < 1).astype(jnp.int32), jax.random.fold_in(streams_of[3], 1), 0, 1)
    w_prev = normal_values(streams_of[4], (L, C, 2 * C), (2 * C) ** -0.5, 0.375)
    w_cur = normal_values(streams_of[5], (L, C, 2 * C), (2 * C) ** -0.5, 0.375)
    w_self = normal_values(streams_of[6], (L, C, C), C ** -0.5, 0.5)
    w_nbr = normal_values(streams_of[7], (L, C, C), C ** -0.5, 0.5)
    dilations = draw_dilations(jax.random.fold_in(streams_of[9], 71), 0)
    return dict(features=features, cotangent=cotangent, tiles=tiles, mask=mask, w_prev=w_prev, w_cur=w_cur, w_self=w_self, w_nbr=w_nbr, dilations=dilations)


def earlier_offset(x, d):
    pad = jnp.zeros((x.shape[0], DD, x.shape[2]), x.dtype)
    paired_terms = jnp.concatenate([pad, x], axis=1)
    return lax.dynamic_slice_in_dim(paired_terms, (DD - d).astype(jnp.int32), DAYS, 1)

def later_offset(x, d):
    pad = jnp.zeros((x.shape[0], DD, x.shape[2]), x.dtype)
    paired_terms = jnp.concatenate([x, pad], axis=1)
    return lax.dynamic_slice_in_dim(paired_terms, d.astype(jnp.int32), DAYS, 1)

def reference(features, cotangent, tiles, mask, w_prev, w_cur, w_self, w_nbr, dilations):
    adjacency = (tiles * mask.astype(tiles.dtype)[:, :, None, None]).transpose(0, 2, 1, 3).reshape(NF, NF)
    saved = []
    hidden_state = features
    for layer_index in range(L):
        dilation_factor = dilations[layer_index]
        previous_state = earlier_offset(hidden_state, dilation_factor)
        pre = jnp.dot(previous_state.reshape(-1, C), w_prev[layer_index], preferred_element_type=jnp.float32)
        pre = pre + jnp.dot(hidden_state.reshape(-1, C), w_cur[layer_index], preferred_element_type=jnp.float32)
        filt = pre[:, :C]
        gate = pre[:, C:]
        gated = (jnp.tanh(filt) * jax.nn.sigmoid(gate)).astype(jnp.bfloat16)
        diffused = jnp.dot(adjacency, gated.reshape(NF, DAYS * C), preferred_element_type=jnp.float32).astype(jnp.bfloat16)
        mixed = jnp.dot(gated, w_self[layer_index], preferred_element_type=jnp.float32)
        mixed = mixed + jnp.dot(diffused.reshape(-1, C), w_nbr[layer_index], preferred_element_type=jnp.float32)
        saved.append((hidden_state, previous_state, filt, gate, gated, diffused))
        hidden_state = (hidden_state.astype(jnp.float32) + mixed.reshape(NF, DAYS, C)).astype(jnp.bfloat16)
    gradient_value = cotangent.astype(jnp.float32)
    outs_prev, outs_cur, outs_self, outs_nbr = ([], [], [], [])
    for layer_index in reversed(range(L)):
        hidden_state, previous_state, filt, gate, gated, diffused = saved[layer_index]
        dilation_factor = dilations[layer_index]
        gzb = gradient_value.astype(jnp.bfloat16).reshape(-1, C)
        outs_self.append(jnp.dot(gated.T, gzb, preferred_element_type=jnp.float32))
        outs_nbr.append(jnp.dot(diffused.reshape(-1, C).T, gzb, preferred_element_type=jnp.float32))
        gdiff = jnp.dot(gzb, w_nbr[layer_index].T, preferred_element_type=jnp.float32).astype(jnp.bfloat16)
        ggated = jnp.dot(gzb, w_self[layer_index].T, preferred_element_type=jnp.float32)
        spread = jnp.dot(adjacency.T, gdiff.reshape(NF, DAYS * C), preferred_element_type=jnp.float32)
        ggated = ggated + spread.reshape(-1, C)
        th = jnp.tanh(filt)
        sg = jax.nn.sigmoid(gate)
        gpre = jnp.concatenate([ggated * sg * (1.0 - th * th), ggated * th * sg * (1.0 - sg)], axis=1).astype(jnp.bfloat16)
        outs_cur.append(jnp.dot(hidden_state.reshape(-1, C).T, gpre, preferred_element_type=jnp.float32))
        outs_prev.append(jnp.dot(previous_state.reshape(-1, C).T, gpre, preferred_element_type=jnp.float32))
        reverse_flow = jnp.dot(gpre, w_prev[layer_index].T, preferred_element_type=jnp.float32).reshape(NF, DAYS, C)
        direct_path = jnp.dot(gpre, w_cur[layer_index].T, preferred_element_type=jnp.float32).reshape(NF, DAYS, C)
        gradient_value = gradient_value + direct_path + later_offset(reverse_flow, dilation_factor)
    factor = 1.0 / jnp.sqrt(jnp.float32(NF * DAYS))
    return (gradient_value, jnp.stack(outs_prev[::-1]) * factor, jnp.stack(outs_cur[::-1]) * factor, jnp.stack(outs_self[::-1]) * factor, jnp.stack(outs_nbr[::-1]) * factor)
```

```python
import jax
import jax.numpy as jnp
from jax import lax
from jax.experimental import pallas as pl
from jax.experimental.pallas import tpu as pltpu
from jax.sharding import PartitionSpec as P

L = 2
NZ = 8
BF = jnp.bfloat16
F32 = jnp.float32

FIRMS = 16
TMS = 16


def along_z(array, by):
    pairs = [(y * NZ + z, y * NZ + (z + by) % NZ) for y in range(2) for z in range(NZ)]
    return lax.ppermute(array, "firm", pairs)


def firm_xor(array, k):
    return lax.ppermute(array, "firm", [(i, i ^ k) for i in range(FIRMS)])


def tm_xor(array, k):
    return lax.ppermute(array, "tm", [(i, i ^ k) for i in range(TMS)])


def along_x(array, by):
    pairs = [(i, ((i // 4 + by) % 4) * 4 + i % 4) for i in range(TMS)]
    return lax.ppermute(array, "tm", pairs)


def along_tm(array, by):
    pairs = [(i, i + by) for i in range(TMS) if 0 <= i + by < TMS]
    return lax.ppermute(array, "tm", pairs)


def mm(a, b, ca=1, cb=0):
    return lax.dot_general(a, b, (((ca,), (cb,)), ((), ())), preferred_element_type=F32)


VMEM_WHOLE = pl.BlockSpec(memory_space=pltpu.VMEM)
SMEM_WHOLE = pl.BlockSpec(memory_space=pltpu.SMEM)


def cost(flops, bytes_accessed):
    return pl.CostEstimate(flops=flops, bytes_accessed=bytes_accessed, transcendentals=0)


def previous_days(near, x_ref, prior_ref, width):
    first = jnp.where(near, prior_ref[:, width:], prior_ref[:, :width])
    second = jnp.where(near, x_ref[:, :width], prior_ref[:, width:])
    return first, second


def gate_kernel(dil_ref, x_ref, prior_ref, wp_ref, wc_ref, gated_ref):
    width = wp_ref.shape[0]
    near = dil_ref[0] == 1
    prevs = previous_days(near, x_ref, prior_ref, width)
    for t in range(2):
        lanes = slice(t * width, (t + 1) * width)
        pre = mm(prevs[t], wp_ref[...]) + mm(x_ref[:, lanes], wc_ref[...])
        gated = jnp.tanh(pre[:, :width]) * jax.nn.sigmoid(pre[:, width:])
        gated_ref[:, lanes] = gated.astype(BF)


def row_spec(block, columns):
    return pl.BlockSpec((block, columns), lambda s: (s, 0))


def whole(shape):
    return pl.BlockSpec(shape, lambda s: (0,) * len(shape))


def gate(dil, x, prior, wp, wc):
    rows, columns = x.shape
    block = rows // 2
    return pl.pallas_call(
        gate_kernel,
        grid=(2,),
        in_specs=[SMEM_WHOLE, row_spec(block, columns), row_spec(block, columns), whole(wp.shape), whole(wc.shape)],
        out_specs=row_spec(block, columns),
        out_shape=jax.ShapeDtypeStruct(x.shape, BF),
        name="gate",
        cost_estimate=cost(2 * rows * 256 * 512, 1 << 20),
    )(dil, x, prior, wp, wc)


def spread_rows(jb_ref, p_ref, g_ref, mask_ref, own_ref, peer_ref, gated_ref, out_own_ref, out_peer_ref, acc_ref):
    s = pl.program_id(0)

    @pl.when(s == 0)
    def _():
        out_own_ref[...] = jnp.zeros_like(out_own_ref)
        acc_ref[...] = jnp.zeros_like(acc_ref)

    piece = gated_ref[0]
    columns = 4 * 16
    for i in range(4):
        rows = slice(i * 128, (i + 1) * 128)
        tiles = []
        for j in range(4):
            keep = mask_ref[i * columns + jb_ref[s] * 4 + j] > 0
            tile = own_ref[i, j]
            tiles.append(jnp.where(keep, tile, jnp.zeros_like(tile)))
        out_own_ref[rows, :] += mm(jnp.concatenate(tiles, axis=1), piece)
        acc_ref[rows, :] += mm(jnp.concatenate([peer_ref[0, i, j] for j in range(4)], axis=1), piece)

    @pl.when(s == pl.num_programs(0) - 1)
    def _():
        out_peer_ref[...] = acc_ref[...].astype(BF)


def spread_forward(jb, pidx, gidx, mask, tiles, peer, stacked):
    rows, columns = stacked.shape[1:]
    return pl.pallas_call(
        spread_rows,
        grid_spec=pltpu.PrefetchScalarGridSpec(
            num_scalar_prefetch=4,
            grid=(NZ,),
            in_specs=[
                pl.BlockSpec((4, 4, 128, 128), lambda s, jb, p, g, m: (0, jb[s], 0, 0)),
                pl.BlockSpec((1, 4, 4, 128, 128), lambda s, jb, p, g, m: (p[s], 0, 0, 0, 0)),
                pl.BlockSpec((1, rows, columns), lambda s, jb, p, g, m: (g[s], 0, 0)),
            ],
            out_specs=[
                pl.BlockSpec((rows, columns), lambda s, jb, p, g, m: (0, 0)),
                pl.BlockSpec((rows, columns), lambda s, jb, p, g, m: (0, 0)),
            ],
            scratch_shapes=[pltpu.VMEM((rows, columns), F32)],
        ),
        out_shape=[jax.ShapeDtypeStruct((rows, columns), F32), jax.ShapeDtypeStruct((rows, columns), BF)],
        name="spread",
        cost_estimate=cost(2 * 1024 * 4096 * 256, 11 << 20),
    )(jb, pidx, gidx, mask, tiles, peer, stacked)


def spread_columns(jb_ref, p_ref, mask_ref, own_ref, peer_ref, mine_ref, theirs_ref, out_ref):
    s = pl.program_id(0)
    columns = 4 * 16
    for half in range(2):
        own, peer = [], []
        for j in (2 * half, 2 * half + 1):
            tiles = []
            for i in range(4):
                keep = mask_ref[i * columns + jb_ref[s] * 4 + j] > 0
                tile = own_ref[i, j]
                tiles.append(jnp.where(keep, tile, jnp.zeros_like(tile)))
            own.append(jnp.concatenate(tiles, axis=0))
            peer.append(jnp.concatenate([peer_ref[0, i, j] for i in range(4)], axis=0))
        total = mm(mine_ref[...], jnp.concatenate(own, axis=1))
        total = total + mm(theirs_ref[...], jnp.concatenate(peer, axis=1))
        out_ref[0, :, half * 256 : (half + 1) * 256] = total


def spread_backward(jb, pidx, mask, tiles, peer, mine, theirs):
    columns, rows = mine.shape
    return pl.pallas_call(
        spread_columns,
        grid_spec=pltpu.PrefetchScalarGridSpec(
            num_scalar_prefetch=3,
            grid=(NZ,),
            in_specs=[
                pl.BlockSpec((4, 4, 128, 128), lambda s, jb, p, m: (0, jb[s], 0, 0)),
                pl.BlockSpec((1, 4, 4, 128, 128), lambda s, jb, p, m: (p[s], 0, 0, 0, 0)),
                pl.BlockSpec((columns, rows), lambda s, jb, p, m: (0, 0)),
                pl.BlockSpec((columns, rows), lambda s, jb, p, m: (0, 0)),
            ],
            out_specs=pl.BlockSpec((1, columns, rows), lambda s, jb, p, m: (s, 0, 0)),
        ),
        out_shape=jax.ShapeDtypeStruct((NZ, columns, rows), F32),
        name="spread_back",
        cost_estimate=cost(2 * 1024 * 4096 * 256, 13 << 20),
    )(jb, pidx, mask, tiles, peer, mine, theirs)


def mix_kernel(x_ref, gated_ref, own_ref, other_ref, ws_ref, wn_ref, out_ref):
    width = ws_ref.shape[0]
    diffused = (own_ref[...] + other_ref[...].astype(F32)).astype(BF)
    for t in range(2):
        lanes = slice(t * width, (t + 1) * width)
        mixed = mm(gated_ref[:, lanes], ws_ref[...]) + mm(diffused[:, lanes], wn_ref[...])
        out_ref[:, lanes] = (x_ref[:, lanes].astype(F32) + mixed).astype(BF)


def mix(x, gated, own, other, ws, wn):
    rows, columns = x.shape
    block = rows // 2
    spec = row_spec(block, columns)
    return pl.pallas_call(
        mix_kernel,
        grid=(2,),
        in_specs=[spec, spec, spec, spec, whole(ws.shape), whole(wn.shape)],
        out_specs=spec,
        out_shape=jax.ShapeDtypeStruct(x.shape, BF),
        name="mix",
        cost_estimate=cost(2 * rows * 256 * 256, 2 << 20),
    )(x, gated, own, other, ws, wn)


def layer_back_kernel(
    dil_ref, x_ref, prior_ref, gz_ref, p_ref, f_ref, b_ref, wp_ref, wc_ref, ws_ref, wn_ref, gx_ref, back_ref, gw_ref
):
    width = ws_ref.shape[0]
    near = dil_ref[0] == 1
    prevs = previous_days(near, x_ref, prior_ref, width)

    @pl.when(pl.program_id(0) == 0)
    def _():
        gw_ref[...] = jnp.zeros_like(gw_ref)

    backs = []
    for t in range(2):
        lanes = slice(t * width, (t + 1) * width)
        x, prev = x_ref[:, lanes], prevs[t]
        pre = mm(prev, wp_ref[...]) + mm(x, wc_ref[...])
        th = jnp.tanh(pre[:, :width])
        sg = jax.nn.sigmoid(pre[:, width:])
        gated = (th * sg).astype(BF)
        gz = gz_ref[:, lanes]
        gzb = gz.astype(BF)
        spread = p_ref[0, lanes, :] + f_ref[lanes, :].astype(F32) + b_ref[lanes, :].astype(F32)
        spread = jnp.transpose(spread).astype(BF)
        ggated = mm(gzb, ws_ref[...], 1, 1) + mm(spread, wn_ref[...], 1, 1)
        gpre = jnp.concatenate(
            [ggated * sg * (1.0 - th * th), ggated * th * sg * (1.0 - sg)], axis=1
        ).astype(BF)
        gw_ref[0:128, :] += mm(gated, gzb, 0, 0)
        gw_ref[128:256, :] += mm(gated, spread, 0, 0)
        gcur = mm(x, gpre, 0, 0)
        gw_ref[256:384, :] += gcur[:, :width]
        gw_ref[384:512, :] += gcur[:, width:]
        gprev = mm(prev, gpre, 0, 0)
        gw_ref[512:640, :] += gprev[:, :width]
        gw_ref[640:768, :] += gprev[:, width:]
        back = mm(gpre, wp_ref[...], 1, 1)
        backs.append(back)
        back_ref[:, lanes] = back.astype(BF)
        gx_ref[:, lanes] = gz.astype(F32) + mm(gpre, wc_ref[...], 1, 1)
    gx_ref[:, :width] += jnp.where(near, backs[1], jnp.zeros_like(backs[1]))


def layer_back(dil, x, prior, gz, parts, f, b, wp, wc, ws, wn):
    rows, columns = x.shape
    block = rows // 2
    spec = row_spec(block, columns)
    turned = pl.BlockSpec((columns, block), lambda s: (0, s))
    return pl.pallas_call(
        layer_back_kernel,
        grid=(2,),
        in_specs=[
            SMEM_WHOLE,
            spec,
            spec,
            spec,
            pl.BlockSpec((1, columns, block), lambda s: (NZ - 1, 0, s)),
            turned,
            turned,
            whole(wp.shape),
            whole(wc.shape),
            whole(ws.shape),
            whole(wn.shape),
        ],
        out_specs=[spec, spec, whole((768, 128))],
        out_shape=[
            jax.ShapeDtypeStruct((rows, columns), F32),
            jax.ShapeDtypeStruct((rows, columns), BF),
            jax.ShapeDtypeStruct((768, 128), F32),
        ],
        name="layer_back",
        cost_estimate=cost(2 * rows * 256 * 2048, 4 << 20),
    )(dil, x, prior, gz, parts, f, b, wp, wc, ws, wn)


def joined(near, gx, later):
    width = gx.shape[1] // 2
    first, second = later[:, :width].astype(F32), later[:, width:].astype(F32)
    shift_first = jnp.where(near, jnp.zeros_like(first), first)
    shift_second = jnp.where(near, first, second)
    return gx[:, :width] + shift_first, gx[:, width:] + shift_second


def join_kernel(dil_ref, gx_ref, later_ref, gz_ref, turned_ref):
    width = gx_ref.shape[1] // 2
    first, second = joined(dil_ref[0] == 1, gx_ref[...], later_ref[...])
    gz_ref[:, :width] = first
    gz_ref[:, width:] = second
    turned_ref[:width, :] = jnp.transpose(first).astype(BF)
    turned_ref[width:, :] = jnp.transpose(second).astype(BF)


def join(dil, gx, later):
    rows, columns = gx.shape
    return pl.pallas_call(
        join_kernel,
        in_specs=[SMEM_WHOLE, VMEM_WHOLE, VMEM_WHOLE],
        out_specs=[VMEM_WHOLE, VMEM_WHOLE],
        out_shape=[jax.ShapeDtypeStruct((rows, columns), F32), jax.ShapeDtypeStruct((columns, rows), BF)],
        name="join",
        cost_estimate=cost(rows * columns * 4, 2 << 20),
    )(dil, gx, later)


def ring_sum(parts):
    half = parts.shape[1] // 2
    send = parts[0].astype(BF)
    f, b = along_z(send[:half], 1), along_z(send[half:], -1)
    ahead = jnp.concatenate([parts[1, :half] + f.astype(F32), parts[1, half:]], axis=0).astype(BF)
    behind = jnp.concatenate([parts[2, :half], parts[2, half:] + b.astype(F32)], axis=0).astype(BF)
    f, b = along_z(ahead, 1), along_z(behind, -1)
    for s in (3, 5):
        ahead = (parts[s] + f.astype(F32)).astype(BF)
        behind = (parts[s + 1] + b.astype(F32)).astype(BF)
        f, b = along_z(ahead, 1), along_z(behind, -1)
    return f, b


def ring_gather(piece):
    half = piece.shape[1] // 2
    f1, b1 = along_z(piece, 1), along_z(piece, -1)
    f2, b2 = along_z(f1, 1), along_z(b1, -1)
    f3, b3 = along_z(f2, 1), along_z(b2, -1)
    f4, b4 = along_z(f3[:, :half], 1), along_z(b3[:, half:], -1)
    return jnp.stack([piece, b1, b2, b3, jnp.concatenate([f4, b4], axis=1), f3, f2, f1])


def sum_four(value, move, step):
    own = value.astype(BF)
    one, two, three = move(own, step), move(own, 2 * step), move(own, 3 * step)
    return (own.astype(F32) + one.astype(F32)) + (two.astype(F32) + three.astype(F32))


def sum_everywhere(weights, x):
    rows = weights.shape[0] // 4
    chunks = weights.reshape(4, rows, weights.shape[1])
    chunks_sent = chunks.astype(BF)
    mine = lax.dynamic_index_in_dim(chunks, x, 0, keepdims=False)
    for k in (1, 2, 3):
        theirs = lax.dynamic_index_in_dim(chunks_sent, x ^ k, 0, keepdims=False)
        mine = mine + tm_xor(theirs, 4 * k).astype(F32)
    mine = sum_four(mine, tm_xor, 1)
    mine = sum_four(mine, firm_xor, 1)
    mine = sum_four(mine, firm_xor, 4)
    mine = mine.astype(BF)
    out = jnp.zeros(chunks.shape, BF)
    out = lax.dynamic_update_index_in_dim(out, mine, x, 0)
    for k in (1, 2, 3):
        out = lax.dynamic_update_index_in_dim(out, tm_xor(mine, 4 * k), x ^ k, 0)
    return out.reshape(weights.shape).astype(F32)


def peer_half(tiles, mask, y, x, core):
    wanted = (1 - y) * NZ + x * 2 + core
    piece = lax.dynamic_slice_in_dim(tiles, wanted * 4, 4, 1)
    kept = lax.dynamic_slice_in_dim(mask, wanted * 4, 4, 1)
    piece = piece * kept.astype(tiles.dtype)[:, :, None, None]
    first = firm_xor(piece, NZ)
    before, after = along_x(first, 1), along_x(first, -1)
    far = jnp.concatenate([along_x(before[:2], 1), along_x(after[2:], -1)], axis=0)
    pieces = [first, after, far, before]
    pieces = pieces + [tm_xor(piece, 1) for piece in pieces]
    return jnp.stack(pieces)


def per_device(features, cotangent, tiles, mask, w_prev, w_cur, w_self, w_nbr, dilations):
    rows, days, width = features.shape
    firm, tm = lax.axis_index("firm"), lax.axis_index("tm")
    y, z = firm // NZ, firm % NZ
    x, core = tm // 4, tm % 2

    def places(offsets):
        q = (z + offsets) % NZ
        where = ((q % 2 - core) % 2) * 4 + (q // 2 - x) % 4
        return (y * NZ + q).astype(jnp.int32), where.astype(jnp.int32)

    flat_mask = mask.reshape(-1)
    gather_order = jnp.arange(NZ, dtype=jnp.int32)
    gather_at = places(gather_order)
    ring_at = places(jnp.array([4, 3, -3, 2, -2, 1, -1, 0], jnp.int32))
    dils = [dilations[layer].reshape(1) for layer in range(L)]

    state = features.reshape(rows, days * width)
    cot = cotangent.reshape(rows, days * width)
    cot_turned = cot.T
    prior = along_tm(state, 1)
    cot_theirs = firm_xor(cot_turned, NZ)
    peer = peer_half(tiles, mask, y, x, core)

    gated = gate(dils[0], state, prior, w_prev[0], w_cur[0])
    stacked = ring_gather(gated)
    own, other = spread_forward(*gather_at, gather_order, flat_mask, tiles, peer, stacked)
    next_state = mix(state, gated, own, firm_xor(other, NZ), w_self[0], w_nbr[0])
    next_prior = along_tm(next_state, 1)

    parts = spread_backward(*ring_at, flat_mask, tiles, peer, cot_turned, cot_theirs)
    f, b = ring_sum(parts)
    gx, back, weights_1 = layer_back(
        dils[1], next_state, next_prior, cot, parts, f, b, w_prev[1], w_cur[1], w_self[1], w_nbr[1]
    )
    gz, gz_turned = join(dils[1], gx, along_tm(back, -1))

    parts = spread_backward(*ring_at, flat_mask, tiles, peer, gz_turned, firm_xor(gz_turned, NZ))
    f, b = ring_sum(parts)
    gx, back, weights_0 = layer_back(
        dils[0], state, prior, gz, parts, f, b, w_prev[0], w_cur[0], w_self[0], w_nbr[0]
    )
    first, second = joined(dils[0][0] == 1, gx, along_tm(back, -1))
    grad = jnp.stack([first, second], axis=1)

    factor = 1.0 / jnp.sqrt(jnp.float32(rows * FIRMS * days * TMS))
    sums = jnp.stack([sum_everywhere(weights_0, x), sum_everywhere(weights_1, x)]) * factor
    g_self, g_nbr = sums[:, 0:128], sums[:, 128:256]
    g_cur = jnp.concatenate([sums[:, 256:384], sums[:, 384:512]], axis=2)
    g_prev = jnp.concatenate([sums[:, 512:640], sums[:, 640:768]], axis=2)
    return grad, g_prev, g_cur, g_self, g_nbr


def solution(mesh):
    in_specs = (
        P("firm", "tm", None),
        P("firm", "tm", None),
        P("firm", None, None, None),
        P("firm", None),
        P(),
        P(),
        P(),
        P(),
        P(),
    )
    out_specs = (P("firm", "tm", None), P(), P(), P(), P())
    return jax.shard_map(per_device, mesh=mesh, in_specs=in_specs, out_specs=out_specs, check_vma=False)
```

```python
import jax
import jax.numpy as jnp
from jax import lax
from jax.experimental import pallas as pl
from jax.experimental.pallas import tpu as pltpu
from jax.sharding import PartitionSpec as P

L = 2
NZ = 8
BF = jnp.bfloat16
F32 = jnp.float32

FIRMS = 16
TMS = 16
ANY = pl.BlockSpec(memory_space=pl.ANY)


def along_z(array, by):
    pairs = [(y * NZ + z, y * NZ + (z + by) % NZ) for y in range(2) for z in range(NZ)]
    return lax.ppermute(array, "firm", pairs)


def firm_xor(array, k):
    return lax.ppermute(array, "firm", [(i, i ^ k) for i in range(FIRMS)])


def tm_xor(array, k):
    return lax.ppermute(array, "tm", [(i, i ^ k) for i in range(TMS)])


def along_x(array, by):
    pairs = [(i, ((i // 4 + by) % 4) * 4 + i % 4) for i in range(TMS)]
    return lax.ppermute(array, "tm", pairs)


def along_tm(array, by):
    pairs = [(i, i + by) for i in range(TMS) if 0 <= i + by < TMS]
    return lax.ppermute(array, "tm", pairs)


def mm(a, b, ca=1, cb=0):
    return lax.dot_general(a, b, (((ca,), (cb,)), ((), ())), preferred_element_type=F32)


VMEM_WHOLE = pl.BlockSpec(memory_space=pltpu.VMEM)
SMEM_WHOLE = pl.BlockSpec(memory_space=pltpu.SMEM)


def cost(flops, bytes_accessed):
    return pl.CostEstimate(flops=flops, bytes_accessed=bytes_accessed, transcendentals=0)


def row_spec(block, columns):
    return pl.BlockSpec((block, columns), lambda s: (s, 0))


def whole(shape):
    return pl.BlockSpec(shape, lambda s: (0,) * len(shape))


def of_layer(weights, layer):
    return pl.BlockSpec((None,) + weights.shape[1:], lambda s: (layer, 0, 0))


def seat(pos):
    return pos // 128, (pos // 16) % 8, (pos // 4) % 4, pos % 2


def masked(mask_ref, tiles_ref, out_ref, block_column):
    for i in range(4):
        for j in range(4):
            tile = tiles_ref[i, j]
            keep = mask_ref[i, block_column * 4 + j] > 0
            out_ref[i * 128 : (i + 1) * 128, j * 128 : (j + 1) * 128] = jnp.where(keep, tile, jnp.zeros_like(tile))


def lent_column(pos):
    y, z, x, core = seat(pos)
    return (1 - y) * NZ + x * 2 + core


def lend_kernel(pos_ref, mask_ref, tiles_ref, out_ref):
    masked(mask_ref, tiles_ref, out_ref, lent_column(pos_ref[0]))


def lend(pos, mask, tiles):
    return pl.pallas_call(
        lend_kernel,
        grid_spec=pltpu.PrefetchScalarGridSpec(
            num_scalar_prefetch=2,
            grid=(1,),
            in_specs=[pl.BlockSpec((4, 4, 128, 128), lambda s, pos, m: (0, lent_column(pos[0]), 0, 0))],
            out_specs=pl.BlockSpec((512, 512), lambda s, pos, m: (0, 0)),
        ),
        out_shape=jax.ShapeDtypeStruct((512, 512), BF),
        name="lend",
        cost_estimate=cost(0, 1 << 20),
    )(pos, mask, tiles)


def prepare_kernel(pos_ref, mask_ref, tiles_ref, cot_ref, out_ref, turned_ref):
    s = pl.program_id(0)
    width = cot_ref.shape[1] // 2
    masked(mask_ref, tiles_ref, out_ref.at[0], seat(pos_ref[0])[0] * NZ + s)

    @pl.when(s == 0)
    def _():
        for t in range(2):
            lanes = slice(t * width, (t + 1) * width)
            turned_ref[lanes, :] = jnp.transpose(cot_ref[:, lanes].astype(F32)).astype(BF)


def prepare(pos, mask, tiles, cot):
    rows, columns = cot.shape
    return pl.pallas_call(
        prepare_kernel,
        grid_spec=pltpu.PrefetchScalarGridSpec(
            num_scalar_prefetch=2,
            grid=(NZ,),
            in_specs=[
                pl.BlockSpec((4, 4, 128, 128), lambda s, pos, m: (0, seat(pos[0])[0] * NZ + s, 0, 0)),
                pl.BlockSpec((rows, columns), lambda s, pos, m: (0, 0)),
            ],
            out_specs=[
                pl.BlockSpec((1, 512, 512), lambda s, pos, m: (s, 0, 0)),
                pl.BlockSpec((columns, rows), lambda s, pos, m: (0, 0)),
            ],
        ),
        out_shape=[jax.ShapeDtypeStruct((NZ, 512, 512), BF), jax.ShapeDtypeStruct((columns, rows), BF)],
        name="prepare",
        cost_estimate=cost(0, 9 << 20),
    )(pos, mask, tiles, cot)


def previous_days(near, x_ref, prior_ref, width):
    first = jnp.where(near, prior_ref[:, width:], prior_ref[:, :width])
    second = jnp.where(near, x_ref[:, :width], prior_ref[:, width:])
    return first, second


def gate_kernel(dil_ref, x_ref, prior_ref, wp_ref, wc_ref, gated_ref):
    width = wp_ref.shape[0]
    near = dil_ref[0] == 1
    prevs = previous_days(near, x_ref, prior_ref, width)
    for t in range(2):
        lanes = slice(t * width, (t + 1) * width)
        pre = mm(prevs[t], wp_ref[...]) + mm(x_ref[:, lanes], wc_ref[...])
        gated = jnp.tanh(pre[:, :width]) * jax.nn.sigmoid(pre[:, width:])
        gated_ref[:, lanes] = gated.astype(BF)


def gate(dil, x, prior, wp, wc):
    rows, columns = x.shape
    block = rows // 2
    return pl.pallas_call(
        gate_kernel,
        grid=(2,),
        in_specs=[SMEM_WHOLE, row_spec(block, columns), row_spec(block, columns), of_layer(wp, 0), of_layer(wc, 0)],
        out_specs=row_spec(block, columns),
        out_shape=jax.ShapeDtypeStruct(x.shape, BF),
        name="gate",
        cost_estimate=cost(2 * rows * 256 * 512, 1 << 20),
    )(dil, x, prior, wp, wc)


PIECES = [(0, 0, 512), (1, 0, 512), (2, 0, 256), (2, 256, 256), (3, 0, 512)]
PIECES = PIECES + [(slot + 4, row, rows) for slot, row, rows in PIECES]
GATHERED = [(0, 0, 256), (1, 0, 256), (2, 0, 256), (3, 0, 256), (4, 0, 128), (4, 128, 128), (5, 0, 256), (6, 0, 256), (7, 0, 256)]


def piece_copies(peer_refs, buffer, sems):
    return [
        pltpu.make_async_copy(ref, buffer.at[slot, pl.ds(row, rows)], sems.at[k])
        for k, (ref, (slot, row, rows)) in enumerate(zip(peer_refs, PIECES))
    ]


def slot_of(q, pos):
    y, z, x, core = seat(pos)
    return ((q + core) % 2) * 4 + (q // 2 - x + 4) % 4


def spread_rows(pos_ref, own_ref, *refs):
    peers, pieces = refs[: len(PIECES)], refs[len(PIECES) : len(PIECES) + len(GATHERED)]
    out_own_ref, out_peer_ref, acc_ref, buffer, gathered, peer_sems, sems = refs[len(PIECES) + len(GATHERED) :]
    s = pl.program_id(0)
    pos = pos_ref[0]

    @pl.when(s == 0)
    def _():
        copies = [
            pltpu.make_async_copy(ref, gathered.at[slot, :, pl.ds(column, columns)], sems.at[k])
            for k, (ref, (slot, column, columns)) in enumerate(zip(pieces, GATHERED))
        ]
        copies = copies + piece_copies(peers, buffer, peer_sems)
        for copy in copies:
            copy.start()
        out_own_ref[...] = jnp.zeros_like(out_own_ref)
        acc_ref[...] = jnp.zeros_like(acc_ref)
        for copy in copies:
            copy.wait()

    piece = gathered[(s - seat(pos)[1] + NZ) % NZ]
    out_own_ref[...] += mm(own_ref[0], piece)
    acc_ref[...] += mm(buffer[slot_of(s, pos)], piece)

    @pl.when(s == pl.num_programs(0) - 1)
    def _():
        out_peer_ref[...] = acc_ref[...].astype(BF)


def spread_forward(pos, mine, peers, pieces):
    rows, columns = pieces[0].shape
    fixed = pl.BlockSpec((rows, columns), lambda s, pos: (0, 0))
    return pl.pallas_call(
        spread_rows,
        grid_spec=pltpu.PrefetchScalarGridSpec(
            num_scalar_prefetch=1,
            grid=(NZ,),
            in_specs=[pl.BlockSpec((1, 512, 512), lambda s, pos: (s, 0, 0))] + [ANY] * (len(PIECES) + len(GATHERED)),
            out_specs=[fixed, fixed],
            scratch_shapes=[
                pltpu.VMEM((rows, columns), F32),
                pltpu.VMEM((NZ, 512, 512), BF),
                pltpu.VMEM((NZ, rows, columns), BF),
                pltpu.SemaphoreType.DMA((len(PIECES),)),
                pltpu.SemaphoreType.DMA((len(GATHERED),)),
            ],
        ),
        out_shape=[jax.ShapeDtypeStruct((rows, columns), F32), jax.ShapeDtypeStruct((rows, columns), BF)],
        name="spread",
        cost_estimate=cost(2 * 1024 * 4096 * 256, 11 << 20),
    )(pos, mine, *peers, *pieces)


def ring_column(s, pos):
    return (seat(pos)[1] + jnp.where(s % 2 == 1, (7 - s) // 2, s // 2 - 4) + NZ) % NZ


def spread_columns(pos_ref, own_ref, mine_ref, theirs_ref, *refs):
    peers = refs[: len(PIECES)]
    first_ref, out_ref, buffer, sems = refs[len(PIECES) :]
    s = pl.program_id(0)
    pos = pos_ref[0]

    @pl.when(s == 0)
    def _():
        copies = piece_copies(peers, buffer, sems)
        for copy in copies:
            copy.start()
        for copy in copies:
            copy.wait()

    total = mm(mine_ref[...], own_ref[0]) + mm(theirs_ref[...], buffer[slot_of(ring_column(s, pos), pos)])

    @pl.when(s == 0)
    def _():
        first_ref[...] = total.astype(BF)

    @pl.when(s > 0)
    def _():
        out_ref[0] = total


def spread_backward(pos, own, peers, mine, theirs):
    columns, rows = mine.shape
    fixed = pl.BlockSpec((columns, rows), lambda s, pos: (0, 0))
    return pl.pallas_call(
        spread_columns,
        grid_spec=pltpu.PrefetchScalarGridSpec(
            num_scalar_prefetch=1,
            grid=(NZ,),
            in_specs=[pl.BlockSpec((1, 512, 512), lambda s, pos: (ring_column(s, pos[0]), 0, 0)), fixed, fixed] + [ANY] * len(PIECES),
            out_specs=[fixed, pl.BlockSpec((1, columns, rows), lambda s, pos: (jnp.maximum(s - 1, 0), 0, 0))],
            scratch_shapes=[pltpu.VMEM((NZ, 512, 512), BF), pltpu.SemaphoreType.DMA((len(PIECES),))],
        ),
        out_shape=[jax.ShapeDtypeStruct((columns, rows), BF), jax.ShapeDtypeStruct((NZ - 1, columns, rows), F32)],
        name="spread_back",
        cost_estimate=cost(2 * 1024 * 4096 * 256, 13 << 20),
    )(pos, own, mine, theirs, *peers)


def mix_kernel(x_ref, gated_ref, own_ref, other_ref, ws_ref, wn_ref, out_ref):
    width = ws_ref.shape[0]
    diffused = (own_ref[...] + other_ref[...].astype(F32)).astype(BF)
    for t in range(2):
        lanes = slice(t * width, (t + 1) * width)
        mixed = mm(gated_ref[:, lanes], ws_ref[...]) + mm(diffused[:, lanes], wn_ref[...])
        out_ref[:, lanes] = (x_ref[:, lanes].astype(F32) + mixed).astype(BF)


def mix(x, gated, own, other, ws, wn):
    rows, columns = x.shape
    block = rows // 2
    spec = row_spec(block, columns)
    return pl.pallas_call(
        mix_kernel,
        grid=(2,),
        in_specs=[spec, spec, spec, spec, of_layer(ws, 0), of_layer(wn, 0)],
        out_specs=spec,
        out_shape=jax.ShapeDtypeStruct(x.shape, BF),
        name="mix",
        cost_estimate=cost(2 * rows * 256 * 256, 2 << 20),
    )(x, gated, own, other, ws, wn)


def layer_back_kernel(
    layer, dil_ref, x_ref, prior_ref, gz_ref, p_ref, f_ref, b_ref, wp_ref, wc_ref, ws_ref, wn_ref, *refs
):
    if layer:
        gx_ref, back_ref, gw_ref = refs
    else:
        upper_ref, gx_ref, back_ref, sent_ref, gw_ref = refs
    width = ws_ref.shape[0]
    near = dil_ref[layer] == 1
    prevs = previous_days(near, x_ref, prior_ref, width)

    @pl.when(pl.program_id(0) == 0)
    def _():
        gw_ref[...] = jnp.zeros_like(gw_ref)

    backs = []
    for t in range(2):
        lanes = slice(t * width, (t + 1) * width)
        x, prev = x_ref[:, lanes], prevs[t]
        pre = mm(prev, wp_ref[...]) + mm(x, wc_ref[...])
        th = jnp.tanh(pre[:, :width])
        sg = jax.nn.sigmoid(pre[:, width:])
        gated = (th * sg).astype(BF)
        gz = gz_ref[:, lanes]
        gzb = gz.astype(BF)
        spread = p_ref[0, lanes, :] + f_ref[lanes, :].astype(F32) + b_ref[lanes, :].astype(F32)
        spread = jnp.transpose(spread).astype(BF)
        ggated = mm(gzb, ws_ref[...], 1, 1) + mm(spread, wn_ref[...], 1, 1)
        gpre = jnp.concatenate(
            [ggated * sg * (1.0 - th * th), ggated * th * sg * (1.0 - sg)], axis=1
        ).astype(BF)
        gw_ref[0:128, :] += mm(gated, gzb, 0, 0)
        gw_ref[128:256, :] += mm(gated, spread, 0, 0)
        gcur = mm(x, gpre, 0, 0)
        gw_ref[256:384, :] += gcur[:, :width]
        gw_ref[384:512, :] += gcur[:, width:]
        gprev = mm(prev, gpre, 0, 0)
        gw_ref[512:640, :] += gprev[:, :width]
        gw_ref[640:768, :] += gprev[:, width:]
        back = mm(gpre, wp_ref[...], 1, 1)
        backs.append(back)
        back_ref[:, lanes] = back.astype(BF)
        gx_ref[:, lanes] = gz.astype(F32) + mm(gpre, wc_ref[...], 1, 1)
    gx_ref[:, :width] += jnp.where(near, backs[1], jnp.zeros_like(backs[1]))
    if not layer:

        @pl.when(pl.program_id(0) == pl.num_programs(0) - 1)
        def _():
            for k in range(8):
                sent_ref[k] = gw_ref[96 * k : 96 * (k + 1), :].astype(BF)
                sent_ref[8 + k] = upper_ref[96 * k : 96 * (k + 1), :].astype(BF)


def layer_back(layer, dil, x, prior, gz, parts, f, b, wp, wc, ws, wn, upper=None):
    rows, columns = x.shape
    block = rows // 2
    spec = row_spec(block, columns)
    turned = pl.BlockSpec((columns, block), lambda s: (0, s))
    gw = jax.ShapeDtypeStruct((768, 128), F32)
    out_specs = [spec, spec, whole(gw.shape)]
    out_shape = [jax.ShapeDtypeStruct((rows, columns), F32), jax.ShapeDtypeStruct((rows, columns), BF), gw]
    if not layer:
        out_specs[2] = whole((TMS, 96, 128))
        out_shape[2] = jax.ShapeDtypeStruct((TMS, 96, 128), BF)
    extra = [] if layer else [upper]
    return pl.pallas_call(
        lambda *refs: layer_back_kernel(layer, *refs),
        grid=(2,),
        in_specs=[
            SMEM_WHOLE,
            spec,
            spec,
            spec,
            pl.BlockSpec((1, columns, block), lambda s: (NZ - 2, 0, s)),
            turned,
            turned,
            of_layer(wp, layer),
            of_layer(wc, layer),
            of_layer(ws, layer),
            of_layer(wn, layer),
        ]
        + [whole(gw.shape) for _ in extra],
        out_specs=out_specs,
        out_shape=out_shape,
        scratch_shapes=[] if layer else [pltpu.VMEM(gw.shape, F32)],
        name="layer_back",
        cost_estimate=cost(2 * rows * 256 * 2048, 4 << 20),
    )(dil, x, prior, gz, parts, f, b, wp, wc, ws, wn, *extra)


def joined(near, gx, later):
    width = gx.shape[1] // 2
    first, second = later[:, :width].astype(F32), later[:, width:].astype(F32)
    shift_first = jnp.where(near, jnp.zeros_like(first), first)
    shift_second = jnp.where(near, first, second)
    return gx[:, :width] + shift_first, gx[:, width:] + shift_second


def join_kernel(dil_ref, gx_ref, later_ref, gz_ref, turned_ref):
    width = gx_ref.shape[1] // 2
    first, second = joined(dil_ref[1] == 1, gx_ref[...], later_ref[...])
    gz_ref[:, :width] = first
    gz_ref[:, width:] = second
    turned_ref[:width, :] = jnp.transpose(first).astype(BF)
    turned_ref[width:, :] = jnp.transpose(second).astype(BF)


def join(dil, gx, later):
    rows, columns = gx.shape
    return pl.pallas_call(
        join_kernel,
        in_specs=[SMEM_WHOLE, VMEM_WHOLE, VMEM_WHOLE],
        out_specs=[VMEM_WHOLE, VMEM_WHOLE],
        out_shape=[jax.ShapeDtypeStruct((rows, columns), F32), jax.ShapeDtypeStruct((columns, rows), BF)],
        name="join",
        cost_estimate=cost(rows * columns * 4, 2 << 20),
    )(dil, gx, later)


def ring_sum(send, parts):
    half = send.shape[0] // 2
    f, b = along_z(send[:half], 1), along_z(send[half:], -1)
    ahead = jnp.concatenate([parts[0, :half] + f.astype(F32), parts[0, half:]], axis=0).astype(BF)
    behind = jnp.concatenate([parts[1, :half], parts[1, half:] + b.astype(F32)], axis=0).astype(BF)
    f, b = along_z(ahead, 1), along_z(behind, -1)
    for s in (2, 4):
        ahead = (parts[s] + f.astype(F32)).astype(BF)
        behind = (parts[s + 1] + b.astype(F32)).astype(BF)
        f, b = along_z(ahead, 1), along_z(behind, -1)
    return f, b


def ring_gather(piece):
    half = piece.shape[1] // 2
    f1, b1 = along_z(piece, 1), along_z(piece, -1)
    f2, b2 = along_z(f1, 1), along_z(b1, -1)
    f3, b3 = along_z(f2, 1), along_z(b2, -1)
    f4, b4 = along_z(f3[:, :half], 1), along_z(b3[:, half:], -1)
    return [piece, b1, b2, b3, f4, b4, f3, f2, f1]


def exchanged(chunks, axis):
    return lax.all_to_all(chunks, axis, 0, 0).astype(F32)


def sum_everywhere(chunks):
    mine = jnp.sum(exchanged(chunks, "tm"), axis=0).astype(BF)
    mine = jnp.sum(exchanged(jnp.broadcast_to(mine, (FIRMS,) + mine.shape), "firm"), axis=0).astype(BF)
    return exchanged(jnp.broadcast_to(mine, chunks.shape), "tm")


def peer_half(first, after_this):
    first, _ = lax.optimization_barrier((first, after_this))
    before, after = along_x(first, 1), along_x(first, -1)
    pieces = [first, after, along_x(before[:256], 1), along_x(after[256:], -1), before]
    return pieces + [tm_xor(piece, 1) for piece in pieces]


def per_device(features, cotangent, tiles, mask, w_prev, w_cur, w_self, w_nbr, dilations):
    rows, days, width = features.shape
    firm, tm = lax.axis_index("firm"), lax.axis_index("tm")
    pos = (firm * TMS + tm).astype(jnp.int32).reshape(1)

    state = features.reshape(rows, days * width)
    cot = cotangent.reshape(rows, days * width)
    prior = along_tm(state, 1)
    lent = firm_xor(lend(pos, mask, tiles), NZ)
    gated = gate(dilations, state, prior, w_prev, w_cur)
    pieces = ring_gather(gated)
    mine, cot_turned = prepare(pos, mask, tiles, cot)
    cot_theirs = firm_xor(cot_turned, NZ)
    peers = peer_half(lent, pieces[-1])

    own, other = spread_forward(pos, mine, peers, pieces)
    next_state = mix(state, gated, own, firm_xor(other, NZ), w_self, w_nbr)
    next_prior = along_tm(next_state, 1)

    send, parts = spread_backward(pos, mine, peers, cot_turned, cot_theirs)
    f, b = ring_sum(send, parts)
    gx, back, upper = layer_back(
        1, dilations, next_state, next_prior, cot, parts, f, b, w_prev, w_cur, w_self, w_nbr
    )
    gz, gz_turned = join(dilations, gx, along_tm(back, -1))

    send, parts = spread_backward(pos, mine, peers, gz_turned, firm_xor(gz_turned, NZ))
    f, b = ring_sum(send, parts)
    gx, back, weights = layer_back(
        0, dilations, state, prior, gz, parts, f, b, w_prev, w_cur, w_self, w_nbr, upper
    )
    first, second = joined(dilations[0] == 1, gx, along_tm(back, -1))
    grad = jnp.stack([first, second], axis=1)

    factor = 1.0 / jnp.sqrt(jnp.float32(rows * FIRMS * days * TMS))
    sums = sum_everywhere(weights).reshape(L, 768, width) * factor
    g_self, g_nbr = sums[:, 0:128], sums[:, 128:256]
    g_cur = jnp.concatenate([sums[:, 256:384], sums[:, 384:512]], axis=2)
    g_prev = jnp.concatenate([sums[:, 512:640], sums[:, 640:768]], axis=2)
    return grad, g_prev, g_cur, g_self, g_nbr


def solution(mesh):
    in_specs = (
        P("firm", "tm", None),
        P("firm", "tm", None),
        P("firm", None, None, None),
        P("firm", None),
        P(),
        P(),
        P(),
        P(),
        P(),
    )
    out_specs = (P("firm", "tm", None), P(), P(), P(), P())
    return jax.shard_map(per_device, mesh=mesh, in_specs=in_specs, out_specs=out_specs, check_vma=False)
```

```python
import jax
import jax.numpy as jnp
from jax import lax
from jax.experimental import pallas as pl
from jax.experimental.pallas import tpu as pltpu
from jax.sharding import PartitionSpec as P


L = 2
NZ = 8
BF = jnp.bfloat16
F32 = jnp.float32

FIRMS = 16
TMS = 16
ANY = pl.BlockSpec(memory_space=pltpu.HBM)


def along_z(array, by):
    pairs = [(y * NZ + z, y * NZ + (z + by) % NZ) for y in range(2) for z in range(NZ)]
    return lax.ppermute(array, "firm", pairs)


def firm_xor(array, k):
    return lax.ppermute(array, "firm", [(i, i ^ k) for i in range(FIRMS)])


def tm_xor(array, k):
    return lax.ppermute(array, "tm", [(i, i ^ k) for i in range(TMS)])


def along_x(array, by):
    pairs = [(i, ((i // 4 + by) % 4) * 4 + i % 4) for i in range(TMS)]
    return lax.ppermute(array, "tm", pairs)


def along_tm(array, by):
    pairs = [(i, i + by) for i in range(TMS) if 0 <= i + by < TMS]
    return lax.ppermute(array, "tm", pairs)


def mm(a, b, ca=1, cb=0):
    return lax.dot_general(a, b, (((ca,), (cb,)), ((), ())), preferred_element_type=F32)


VMEM_WHOLE = pl.BlockSpec(memory_space=pltpu.VMEM)
SMEM_WHOLE = pl.BlockSpec(memory_space=pltpu.SMEM)


def whole_call(kernel, outs, ins, flops=0, bytes_accessed=1 << 20, scratch=(), grant=16 << 20):
    return pl.pallas_call(
        kernel,
        in_specs=[spec for _, spec in ins],
        out_specs=[VMEM_WHOLE for _ in outs],
        out_shape=[jax.ShapeDtypeStruct(shape, dtype) for shape, dtype in outs],
        scratch_shapes=list(scratch),
        cost_estimate=cost(flops, bytes_accessed),
        compiler_params=pltpu.CompilerParams(vmem_limit_bytes=grant),
    )(*[array for array, _ in ins])


def behind(array, *earlier):
    return lax.optimization_barrier((array,) + earlier)[0]


def cost(flops, bytes_accessed):
    return pl.CostEstimate(flops=flops, bytes_accessed=bytes_accessed, transcendentals=0)


def seat(pos):
    return pos // 128, (pos // 16) % 8, (pos // 4) % 4, pos % 2


def fetch(mask_ref, tiles_ref, target, sems, slot, block_column):
    copies = []
    for i in range(4):
        for j in range(4):
            copies.append(
                pltpu.make_async_copy(
                    tiles_ref.at[i, block_column * 4 + j],
                    target.at[i * 128 : (i + 1) * 128, j * 128 : (j + 1) * 128],
                    sems.at[slot, i * 4 + j],
                )
            )

    def finish():
        for copy in copies:
            copy.wait()
        for i in range(4):
            for j in range(4):

                @pl.when(mask_ref[i, block_column * 4 + j] == 0)
                def _():
                    target[i * 128 : (i + 1) * 128, j * 128 : (j + 1) * 128] = jnp.zeros((128, 128), BF)

    return copies, finish


def lend_kernel(pos_ref, mask_ref, tiles_ref, out_ref, sems):
    y, _, x, core = seat(pos_ref[0])
    copies, finish = fetch(mask_ref, tiles_ref, out_ref, sems, 0, (1 - y) * NZ + x * 2 + core)
    for copy in copies:
        copy.start()
    finish()


def lend(pos, mask, tiles):
    return whole_call(
        lend_kernel,
        [((512, 512), BF)],
        [(pos, SMEM_WHOLE), (mask, SMEM_WHOLE), (tiles, ANY)],
        scratch=[pltpu.SemaphoreType.DMA((1, 16))],
        grant=53 << 20,
    )[0]


def prepare_kernel(pos_ref, mask_ref, cot_ref, tiles_ref, out_ref, turned_ref, sems):
    width = cot_ref.shape[1] // 2
    base = seat(pos_ref[0])[0] * NZ

    def start(q, carry):
        for copy in fetch(mask_ref, tiles_ref, out_ref.at[q], sems, q, base + q)[0]:
            copy.start()
        return carry

    def finish(q, carry):
        fetch(mask_ref, tiles_ref, out_ref.at[q], sems, q, base + q)[1]()
        return carry

    lax.fori_loop(0, NZ, start, 0)
    for t in range(2):
        lanes = slice(t * width, (t + 1) * width)
        turned_ref[lanes, :] = jnp.transpose(cot_ref[:, lanes].astype(F32)).astype(BF)
    lax.fori_loop(0, NZ, finish, 0)


def prepare(pos, mask, tiles, cot):
    rows, columns = cot.shape
    return whole_call(
        prepare_kernel,
        [((NZ, 512, 512), BF), ((columns, rows), BF)],
        [(pos, SMEM_WHOLE), (mask, SMEM_WHOLE), (cot, VMEM_WHOLE), (tiles, ANY)],
        bytes_accessed=9 << 20,
        scratch=[pltpu.SemaphoreType.DMA((NZ, 16))],
        grant=53 << 20,
    )


def previous_days(near, x, prior):
    width = x.shape[1] // 2
    first = jnp.where(near, prior[:, width:], prior[:, :width])
    second = jnp.where(near, x[:, :width], prior[:, width:])
    return first, second


def halves(array):
    width = array.shape[1] // 2
    return array[:, :width], array[:, width:]


BLOCK = 256


def by_blocks(rows, body):
    def step(s, carry):
        body(pl.ds(pl.multiple_of(s * BLOCK, BLOCK), BLOCK))
        return carry

    lax.fori_loop(0, rows // BLOCK, step, 0)


def gate_kernel(dil_ref, x_ref, prior_ref, wp_ref, wc_ref, gated_ref):
    width = wp_ref.shape[1]
    near = dil_ref[0] == 1

    def body(rows):
        x = x_ref[rows, :]
        prevs = previous_days(near, x, prior_ref[rows, :])
        for t in range(2):
            lanes = slice(t * width, (t + 1) * width)
            pre = mm(prevs[t], wp_ref[0]) + mm(x[:, lanes], wc_ref[0])
            gated_ref[rows, lanes] = (jnp.tanh(pre[:, :width]) * jax.nn.sigmoid(pre[:, width:])).astype(BF)

    by_blocks(x_ref.shape[0], body)


def gate(dil, x, prior, wp, wc):
    return whole_call(
        gate_kernel,
        [(x.shape, BF)],
        [(dil, SMEM_WHOLE), (x, VMEM_WHOLE), (prior, VMEM_WHOLE), (wp, VMEM_WHOLE), (wc, VMEM_WHOLE)],
        flops=2 * 512 * 256 * 512,
    )[0]


def gather_kernel(pos_ref, first_ref, sides_ref, far0_ref, far1_ref, other_ref, other_sides_ref, other_far_ref, out_ref):
    _, _, x, core = seat(pos_ref[0])

    def column(step, sibling):
        return ((x + step) % 4) * 2 + (core if not sibling else 1 - core)

    out_ref[column(0, False)] = first_ref[...]
    out_ref[column(1, False)] = sides_ref[:512]
    out_ref[column(3, False)] = sides_ref[512:]
    out_ref[column(2, False), :256] = far0_ref[...]
    out_ref[column(2, False), 256:] = far1_ref[...]
    out_ref[column(0, True)] = other_ref[...]
    out_ref[column(1, True)] = other_sides_ref[:512]
    out_ref[column(3, True)] = other_sides_ref[512:]
    out_ref[column(2, True)] = other_far_ref[...]


def gather_pieces(pos, pieces):
    return whole_call(
        gather_kernel,
        [((NZ, 512, 512), BF)],
        [(pos, SMEM_WHOLE)] + [(piece, VMEM_WHOLE) for piece in pieces],
        bytes_accessed=8 << 20,
    )[0]


def spread_rows(pos_ref, own_ref, peer_ref, *refs):
    pieces, (out_own_ref, out_peer_ref, acc_ref, gathered) = refs[:9], refs[9:]
    z = seat(pos_ref[0])[1]
    for slot, ref in zip((0, 1, 2, 3, None, None, 5, 6, 7), pieces):
        if slot is not None:
            gathered[slot] = ref[...]
    gathered[4, :, :128] = pieces[4][...]
    gathered[4, :, 128:] = pieces[5][...]
    out_own_ref[...] = jnp.zeros_like(out_own_ref)
    acc_ref[...] = jnp.zeros_like(acc_ref)

    def step(q, carry):
        piece = gathered[(q - z + NZ) % NZ]
        out_own_ref[...] += mm(own_ref[q], piece)
        acc_ref[...] += mm(peer_ref[q], piece)
        return carry

    lax.fori_loop(0, NZ, step, 0)
    out_peer_ref[...] = acc_ref[...].astype(BF)


def spread_forward(pos, own, peer, pieces):
    shape = pieces[0].shape
    return whole_call(
        spread_rows,
        [(shape, F32), (shape, BF)],
        [(pos, SMEM_WHOLE), (own, VMEM_WHOLE), (peer, VMEM_WHOLE)] + [(piece, VMEM_WHOLE) for piece in pieces],
        flops=2 * 1024 * 4096 * 256,
        scratch=[pltpu.VMEM(shape, F32), pltpu.VMEM((NZ,) + shape, BF)],
    )


def ring_column(s, z):
    return (z + jnp.where(s % 2 == 1, (7 - s) // 2, s // 2 - 4) + NZ) % NZ


def spread_columns(pos_ref, own_ref, peer_ref, mine_ref, theirs_ref, first_ref, out_ref, last_ref):
    z = seat(pos_ref[0])[1]

    def step(s, carry):
        q = ring_column(s, z)
        total = mm(mine_ref[...], own_ref[q]) + mm(theirs_ref[...], peer_ref[q])

        @pl.when(s == 0)
        def _():
            first_ref[...] = total.astype(BF)

        @pl.when((s > 0) & (s < NZ - 1))
        def _():
            out_ref[jnp.clip(s - 1, 0, NZ - 3)] = total

        @pl.when(s == NZ - 1)
        def _():
            last_ref[...] = total

        return carry

    lax.fori_loop(0, NZ, step, 0)


def spread_backward(pos, own, peer, mine, theirs):
    shape = mine.shape
    return whole_call(
        spread_columns,
        [(shape, BF), ((NZ - 2,) + shape, F32), (shape, F32)],
        [(pos, SMEM_WHOLE), (own, VMEM_WHOLE), (peer, VMEM_WHOLE), (mine, VMEM_WHOLE), (theirs, VMEM_WHOLE)],
        flops=2 * 1024 * 4096 * 256,
    )


def mix_kernel(x_ref, gated_ref, own_ref, other_ref, ws_ref, wn_ref, out_ref):
    width = ws_ref.shape[1]

    def body(rows):
        diffused = (own_ref[rows, :] + other_ref[rows, :].astype(F32)).astype(BF)
        for t in range(2):
            lanes = slice(t * width, (t + 1) * width)
            mixed = mm(gated_ref[rows, lanes], ws_ref[0]) + mm(diffused[:, lanes], wn_ref[0])
            out_ref[rows, lanes] = (x_ref[rows, lanes].astype(F32) + mixed).astype(BF)

    by_blocks(x_ref.shape[0], body)


def mix(*arrays):
    return whole_call(
        mix_kernel, [(arrays[0].shape, BF)], [(array, VMEM_WHOLE) for array in arrays], flops=2 * 512 * 256 * 256
    )[0]


def layer_back_kernel(
    layer, dil_ref, x_ref, prior_ref, gz_ref, p_ref, f_ref, b_ref, wp_ref, wc_ref, ws_ref, wn_ref, *refs
):
    if layer:
        gx_ref, back_ref, gw_ref = refs
    else:
        upper_ref, gx_ref, back_ref, sent_ref, gw_ref = refs
    width = ws_ref.shape[1]
    near = dil_ref[layer] == 1
    wp, wc, ws, wn = wp_ref.at[layer], wc_ref.at[layer], ws_ref.at[layer], wn_ref.at[layer]
    gw_ref[...] = jnp.zeros_like(gw_ref)

    def body(rows):
        prevs = previous_days(near, x_ref[rows, :], prior_ref[rows, :])
        backs = []
        for t in range(2):
            lanes = slice(t * width, (t + 1) * width)
            x, prev = x_ref[rows, lanes], prevs[t]
            pre = mm(prev, wp[...]) + mm(x, wc[...])
            th = jnp.tanh(pre[:, :width])
            sg = jax.nn.sigmoid(pre[:, width:])
            gated = (th * sg).astype(BF)
            gz = gz_ref[rows, lanes]
            gzb = gz.astype(BF)
            spread = p_ref[lanes, rows] + f_ref[lanes, rows].astype(F32) + b_ref[lanes, rows].astype(F32)
            spread = jnp.transpose(spread).astype(BF)
            ggated = mm(gzb, ws[...], 1, 1) + mm(spread, wn[...], 1, 1)
            gpre = jnp.concatenate(
                [ggated * sg * (1.0 - th * th), ggated * th * sg * (1.0 - sg)], axis=1
            ).astype(BF)
            gw_ref[0:128, :] += mm(gated, gzb, 0, 0)
            gw_ref[128:256, :] += mm(gated, spread, 0, 0)
            gcur = mm(x, gpre, 0, 0)
            gw_ref[256:384, :] += gcur[:, :width]
            gw_ref[384:512, :] += gcur[:, width:]
            gprev = mm(prev, gpre, 0, 0)
            gw_ref[512:640, :] += gprev[:, :width]
            gw_ref[640:768, :] += gprev[:, width:]
            back = mm(gpre, wp[...], 1, 1)
            backs.append(back)
            back_ref[rows, lanes] = back.astype(BF)
            gx_ref[rows, lanes] = gz.astype(F32) + mm(gpre, wc[...], 1, 1)
        gx_ref[rows, :width] += jnp.where(near, backs[1], jnp.zeros_like(backs[1]))

    by_blocks(x_ref.shape[0], body)
    if not layer:
        for k in range(8):
            sent_ref[k] = gw_ref[96 * k : 96 * (k + 1), :].astype(BF)
            sent_ref[8 + k] = upper_ref[96 * k : 96 * (k + 1), :].astype(BF)


def layer_back(layer, dil, arrays, upper=None):
    shape = arrays[0].shape
    outs = [(shape, F32), (shape, BF), ((768, 128), F32)]
    if not layer:
        outs[2] = ((TMS, 96, 128), BF)
        arrays = arrays + [upper]
    return whole_call(
        lambda *refs: layer_back_kernel(layer, *refs),
        outs,
        [(dil, SMEM_WHOLE)] + [(array, VMEM_WHOLE) for array in arrays],
        flops=2 * 512 * 256 * 2048,
        bytes_accessed=4 << 20,
        scratch=[] if layer else [pltpu.VMEM((768, 128), F32)],
    )


def joined(near, gx, later):
    (gx_first, gx_second), (first, second) = halves(gx), halves(later)
    first, second = first.astype(F32), second.astype(F32)
    shift_first = jnp.where(near, jnp.zeros_like(first), first)
    shift_second = jnp.where(near, first, second)
    return gx_first.astype(F32) + shift_first, gx_second.astype(F32) + shift_second


def join_kernel(dil_ref, gx_ref, later_ref, gx_pair_ref, later_pair_ref, gz_ref, turned_ref, turned_pair_ref):
    near = dil_ref[1] == 1
    width = gx_ref.shape[1] // 2
    days = joined(near, gx_ref[...], later_ref[...])
    for t in range(2):
        lanes = slice(t * width, (t + 1) * width)
        gz_ref[:, lanes] = days[t]
        turned_ref[lanes, :] = jnp.transpose(days[t]).astype(BF)
    days = joined(near, gx_pair_ref[...], later_pair_ref[...])
    for t in range(2):
        turned_pair_ref[t * width : (t + 1) * width, :] = jnp.transpose(days[t]).astype(BF)


def join(dil, *arrays):
    rows, columns = arrays[0].shape
    return whole_call(
        join_kernel,
        [((rows, columns), F32), ((columns, rows), BF), ((columns, rows), BF)],
        [(dil, SMEM_WHOLE)] + [(array, VMEM_WHOLE) for array in arrays],
    )


def ring_sum(send, parts, second=None, third=None):
    half = send.shape[0] // 2
    f, b = along_z(send[:half], 1), along_z(send[half:], -1)
    f, b = lax.optimization_barrier((f, b))
    ahead = jnp.concatenate([parts[0, :half] + f.astype(F32), parts[0, half:]], axis=0).astype(BF)
    aback = jnp.concatenate([parts[1, :half], parts[1, half:] + b.astype(F32)], axis=0).astype(BF)
    for s, wait in ((2, second), (4, third)):
        if wait is not None:
            ahead, aback, _ = lax.optimization_barrier((ahead, aback, wait))
        f, b = lax.optimization_barrier((along_z(ahead, 1), along_z(aback, -1)))
        ahead = (parts[s] + f.astype(F32)).astype(BF)
        aback = (parts[s + 1] + b.astype(F32)).astype(BF)
    return along_z(ahead, 1), along_z(aback, -1)


def exchanged(chunks, axis):
    return lax.all_to_all(chunks, axis, 0, 0).astype(F32)


def sum_everywhere(chunks):
    mine = jnp.sum(exchanged(chunks, "tm"), axis=0).astype(BF)
    mine = jnp.sum(exchanged(jnp.broadcast_to(mine, (FIRMS,) + mine.shape), "firm"), axis=0).astype(BF)
    return exchanged(jnp.broadcast_to(mine, chunks.shape), "tm")


def from_pair_later(array):
    pairs = [((i ^ NZ) * TMS + t, i * TMS + t - 1) for i in range(FIRMS) for t in range(1, TMS)]
    return lax.ppermute(array, ("firm", "tm"), pairs)


def per_device(features, cotangent, tiles, mask, w_prev, w_cur, w_self, w_nbr, dilations):
    rows, days, width = features.shape
    firm, tm = lax.axis_index("firm"), lax.axis_index("tm")
    pos = (firm * TMS + tm).astype(jnp.int32).reshape(1)
    weights = [w_prev, w_cur, w_self, w_nbr]

    state = features.reshape(rows, days * width)
    cot = cotangent.reshape(rows, days * width)
    prior = along_tm(state, 1)
    lent = firm_xor(lend(pos, mask, tiles), NZ)
    gated = gate(dilations, state, prior, w_prev, w_cur)

    half = width
    f1, b1 = along_z(gated, 1), along_z(gated, -1)
    own, cot_turned = prepare(behind(pos, gated), mask, tiles, cot)
    f1, b1, own = lax.optimization_barrier((f1, b1, own))
    f2, b2 = along_z(f1, 1), along_z(b1, -1)
    cot_pair = firm_xor(cot_turned, NZ)
    first = behind(lent, f1)
    before, after = along_x(first, 1), along_x(first, -1)
    other_first = tm_xor(first, 1)
    f2, b2, cot_pair = lax.optimization_barrier((f2, b2, cot_pair))
    f3, b3 = along_z(f2, 1), along_z(b2, -1)
    before, after = behind(before, f3, b3), behind(after, f3, b3)
    f4, b4 = along_z(f3[:, :half], 1), along_z(b3[:, half:], -1)
    far = [along_x(before[:256], 1), along_x(after[256:], -1)]
    sides = jnp.concatenate([after, before], axis=0)
    other_sides = tm_xor(sides, 1)
    other_far = tm_xor(jnp.concatenate(far, axis=0), 1)
    peer = gather_pieces(pos, [first, sides] + far + [other_first, other_sides, other_far])
    pieces = [gated, b1, b2, b3, f4, b4, f3, f2, f1]

    send, parts, last = spread_backward(pos, own, peer, cot_turned, cot_pair)
    mixed, other = spread_forward(behind(pos, send), own, peer, pieces)
    next_state = mix(state, gated, mixed, firm_xor(other, NZ), w_self, w_nbr)
    next_prior = along_tm(next_state, 1)
    f, b = ring_sum(send, parts, mixed, next_state)
    gx, back, upper = layer_back(1, dilations, [next_state, next_prior, cot, last, f, b] + weights)

    gx_pair = firm_xor(gx.astype(BF), NZ)
    gz, gz_turned, gz_pair = join(dilations, gx, along_tm(back, -1), gx_pair, from_pair_later(back))
    send, parts, last = spread_backward(pos, own, peer, gz_turned, gz_pair)
    f, b = ring_sum(send, parts)
    gx, back, sent = layer_back(0, dilations, [state, prior, gz, last, f, b] + weights, upper)
    grad = jnp.stack(joined(dilations[0] == 1, gx, along_tm(back, -1)), axis=1)

    factor = 1.0 / jnp.sqrt(jnp.float32(rows * FIRMS * days * TMS))
    sums = sum_everywhere(sent).reshape(L, 768, width) * factor
    g_self, g_nbr = sums[:, 0:128], sums[:, 128:256]
    g_cur = jnp.concatenate([sums[:, 256:384], sums[:, 384:512]], axis=2)
    g_prev = jnp.concatenate([sums[:, 512:640], sums[:, 640:768]], axis=2)
    return grad, g_prev, g_cur, g_self, g_nbr


def solution(mesh):
    in_specs = (
        P("firm", "tm", None),
        P("firm", "tm", None),
        P("firm", None, None, None),
        P("firm", None),
        P(),
        P(),
        P(),
        P(),
        P(),
    )
    out_specs = (P("firm", "tm", None), P(), P(), P(), P())
    return jax.shard_map(per_device, mesh=mesh, in_specs=in_specs, out_specs=out_specs, check_vma=False)
```

```python
import jax
import jax.numpy as jnp
from jax import lax
from jax.experimental import pallas as pl
from jax.experimental.pallas import tpu as pltpu
from jax.sharding import PartitionSpec as P


L = 2
NZ = 8
BF = jnp.bfloat16
F32 = jnp.float32

FIRMS = 16
TMS = 16
ANY = pl.BlockSpec(memory_space=pltpu.HBM)


def along_z(array, by):
    pairs = [(y * NZ + z, y * NZ + (z + by) % NZ) for y in range(2) for z in range(NZ)]
    return lax.ppermute(array, "firm", pairs)


def firm_xor(array, k):
    return lax.ppermute(array, "firm", [(i, i ^ k) for i in range(FIRMS)])


def tm_xor(array, k):
    return lax.ppermute(array, "tm", [(i, i ^ k) for i in range(TMS)])


def along_x(array, by):
    pairs = [(i, ((i // 4 + by) % 4) * 4 + i % 4) for i in range(TMS)]
    return lax.ppermute(array, "tm", pairs)


def along_tm(array, by):
    pairs = [(i, i + by) for i in range(TMS) if 0 <= i + by < TMS]
    return lax.ppermute(array, "tm", pairs)


def mm(a, b, ca=1, cb=0):
    return lax.dot_general(a, b, (((ca,), (cb,)), ((), ())), preferred_element_type=F32)


VMEM_WHOLE = pl.BlockSpec(memory_space=pltpu.VMEM)
SMEM_WHOLE = pl.BlockSpec(memory_space=pltpu.SMEM)


def whole_call(kernel, outs, ins, flops=0, bytes_accessed=1 << 20, scratch=(), grant=16 << 20):
    return pl.pallas_call(
        kernel,
        in_specs=[spec for _, spec in ins],
        out_specs=[VMEM_WHOLE for _ in outs],
        out_shape=[jax.ShapeDtypeStruct(shape, dtype) for shape, dtype in outs],
        scratch_shapes=list(scratch),
        cost_estimate=cost(flops, bytes_accessed),
        compiler_params=pltpu.CompilerParams(vmem_limit_bytes=grant),
    )(*[array for array, _ in ins])


def behind(array, *earlier):
    return lax.optimization_barrier((array,) + earlier)[0]


def cost(flops, bytes_accessed):
    return pl.CostEstimate(flops=flops, bytes_accessed=bytes_accessed, transcendentals=0)


def seat(pos):
    return pos // 128, (pos // 16) % 8, (pos // 4) % 4, pos % 2


def fetch(mask_ref, tiles_ref, target, sems, slot, block_column):
    copies = []
    for i in range(4):
        for j in range(4):
            copies.append(
                pltpu.make_async_copy(
                    tiles_ref.at[i, block_column * 4 + j],
                    target.at[i * 128 : (i + 1) * 128, j * 128 : (j + 1) * 128],
                    sems.at[slot, i * 4 + j],
                )
            )

    def finish():
        for copy in copies:
            copy.wait()
        for i in range(4):
            for j in range(4):

                @pl.when(mask_ref[i, block_column * 4 + j] == 0)
                def _():
                    target[i * 128 : (i + 1) * 128, j * 128 : (j + 1) * 128] = jnp.zeros((128, 128), BF)

    return copies, finish


def lend_kernel(pos_ref, mask_ref, tiles_ref, out_ref, sems):
    y, _, x, core = seat(pos_ref[0])
    copies, finish = fetch(mask_ref, tiles_ref, out_ref, sems, 0, (1 - y) * NZ + x * 2 + core)
    for copy in copies:
        copy.start()
    finish()


def lend(pos, mask, tiles):
    return whole_call(
        lend_kernel,
        [((512, 512), BF)],
        [(pos, SMEM_WHOLE), (mask, SMEM_WHOLE), (tiles, ANY)],
        scratch=[pltpu.SemaphoreType.DMA((1, 16))],
        grant=49 << 20,
    )[0]


def prepare_kernel(pos_ref, mask_ref, cot_ref, tiles_ref, out_ref, turned_ref, sems):
    width = cot_ref.shape[1] // 2
    base = seat(pos_ref[0])[0] * NZ

    def start(q, carry):
        for copy in fetch(mask_ref, tiles_ref, out_ref.at[q], sems, q, base + q)[0]:
            copy.start()
        return carry

    def finish(q, carry):
        fetch(mask_ref, tiles_ref, out_ref.at[q], sems, q, base + q)[1]()
        return carry

    lax.fori_loop(0, NZ, start, 0)
    for t in range(2):
        lanes = slice(t * width, (t + 1) * width)
        turned_ref[lanes, :] = jnp.transpose(cot_ref[:, lanes].astype(F32)).astype(BF)
    lax.fori_loop(0, NZ, finish, 0)


def prepare(pos, mask, tiles, cot):
    rows, columns = cot.shape
    return whole_call(
        prepare_kernel,
        [((NZ, 512, 512), BF), ((columns, rows), BF)],
        [(pos, SMEM_WHOLE), (mask, SMEM_WHOLE), (cot, VMEM_WHOLE), (tiles, ANY)],
        bytes_accessed=9 << 20,
        scratch=[pltpu.SemaphoreType.DMA((NZ, 16))],
        grant=49 << 20,
    )


def previous_days(near, x, prior):
    width = x.shape[1] // 2
    first = jnp.where(near, prior[:, width:], prior[:, :width])
    second = jnp.where(near, x[:, :width], prior[:, width:])
    return first, second


def halves(array):
    width = array.shape[1] // 2
    return array[:, :width], array[:, width:]


BLOCK = 256


def by_blocks(rows, body):
    def step(s, carry):
        body(pl.ds(pl.multiple_of(s * BLOCK, BLOCK), BLOCK))
        return carry

    lax.fori_loop(0, rows // BLOCK, step, 0)


def gate_kernel(dil_ref, x_ref, prior_ref, wp_ref, wc_ref, gated_ref):
    width = wp_ref.shape[1]
    near = dil_ref[0] == 1

    def body(rows):
        x = x_ref[rows, :]
        prevs = previous_days(near, x, prior_ref[rows, :])
        for t in range(2):
            lanes = slice(t * width, (t + 1) * width)
            pre = mm(prevs[t], wp_ref[0]) + mm(x[:, lanes], wc_ref[0])
            gated_ref[rows, lanes] = (jnp.tanh(pre[:, :width]) * jax.nn.sigmoid(pre[:, width:])).astype(BF)

    by_blocks(x_ref.shape[0], body)


def gate(dil, x, prior, wp, wc):
    return whole_call(
        gate_kernel,
        [(x.shape, BF)],
        [(dil, SMEM_WHOLE), (x, VMEM_WHOLE), (prior, VMEM_WHOLE), (wp, VMEM_WHOLE), (wc, VMEM_WHOLE)],
        flops=2 * 512 * 256 * 512,
    )[0]


def gather_kernel(pos_ref, first_ref, sides_ref, far0_ref, far1_ref, other_ref, other_sides_ref, other_far_ref, out_ref):
    _, _, x, core = seat(pos_ref[0])

    def column(step, sibling):
        return ((x + step) % 4) * 2 + (core if not sibling else 1 - core)

    out_ref[column(0, False)] = first_ref[...]
    out_ref[column(1, False)] = sides_ref[:512]
    out_ref[column(3, False)] = sides_ref[512:]
    out_ref[column(2, False), :256] = far0_ref[...]
    out_ref[column(2, False), 256:] = far1_ref[...]
    out_ref[column(0, True)] = other_ref[...]
    out_ref[column(1, True)] = other_sides_ref[:512]
    out_ref[column(3, True)] = other_sides_ref[512:]
    out_ref[column(2, True)] = other_far_ref[...]


def gather_pieces(pos, pieces):
    return whole_call(
        gather_kernel,
        [((NZ, 512, 512), BF)],
        [(pos, SMEM_WHOLE)] + [(piece, VMEM_WHOLE) for piece in pieces],
        bytes_accessed=8 << 20,
    )[0]


def spread_rows(pos_ref, own_ref, peer_ref, *refs):
    pieces, (out_own_ref, out_peer_ref, acc_ref, gathered) = refs[:9], refs[9:]
    z = seat(pos_ref[0])[1]
    for slot, ref in zip((0, 1, 2, 3, None, None, 5, 6, 7), pieces):
        if slot is not None:
            gathered[slot] = ref[...]
    gathered[4, :, :128] = pieces[4][...]
    gathered[4, :, 128:] = pieces[5][...]
    out_own_ref[...] = jnp.zeros_like(out_own_ref)
    acc_ref[...] = jnp.zeros_like(acc_ref)

    def step(q, carry):
        piece = gathered[(q - z + NZ) % NZ]
        out_own_ref[...] += mm(own_ref[q], piece)
        acc_ref[...] += mm(peer_ref[q], piece)
        return carry

    lax.fori_loop(0, NZ, step, 0)
    out_peer_ref[...] = acc_ref[...].astype(BF)


def spread_forward(pos, own, peer, pieces):
    shape = pieces[0].shape
    return whole_call(
        spread_rows,
        [(shape, F32), (shape, BF)],
        [(pos, SMEM_WHOLE), (own, VMEM_WHOLE), (peer, VMEM_WHOLE)] + [(piece, VMEM_WHOLE) for piece in pieces],
        flops=2 * 1024 * 4096 * 256,
        scratch=[pltpu.VMEM(shape, F32), pltpu.VMEM((NZ,) + shape, BF)],
    )


def ring_column(s, z):
    return (z + jnp.where(s % 2 == 1, (7 - s) // 2, s // 2 - 4) + NZ) % NZ


def spread_first(pos_ref, own_ref, peer_ref, mine_ref, theirs_ref, first_ref):
    q = ring_column(0, seat(pos_ref[0])[1])
    first_ref[...] = (mm(mine_ref[...], own_ref[q]) + mm(theirs_ref[...], peer_ref[q])).astype(BF)


def spread_columns(pos_ref, own_ref, peer_ref, mine_ref, theirs_ref, out_ref, last_ref):
    z = seat(pos_ref[0])[1]

    def step(s, carry):
        q = ring_column(s, z)
        total = mm(mine_ref[...], own_ref[q]) + mm(theirs_ref[...], peer_ref[q])

        @pl.when(s < NZ - 1)
        def _():
            out_ref[jnp.minimum(s - 1, NZ - 3)] = total

        @pl.when(s == NZ - 1)
        def _():
            last_ref[...] = total

        return carry

    lax.fori_loop(1, NZ, step, 0)


def spread_backward(pos, own, peer, mine, theirs):
    shape = mine.shape
    ins = [(pos, SMEM_WHOLE), (own, VMEM_WHOLE), (peer, VMEM_WHOLE), (mine, VMEM_WHOLE), (theirs, VMEM_WHOLE)]
    send = whole_call(spread_first, [(shape, BF)], ins, flops=2 * 1024 * 512 * 256)[0]
    ins[0] = (behind(pos, send), SMEM_WHOLE)
    outs = [((NZ - 2,) + shape, F32), (shape, F32)]
    parts, last = whole_call(spread_columns, outs, ins, flops=2 * 1024 * 3584 * 256)
    return send, parts, last


def mix_kernel(x_ref, gated_ref, own_ref, other_ref, ws_ref, wn_ref, out_ref):
    width = ws_ref.shape[1]

    def body(rows):
        diffused = (own_ref[rows, :] + other_ref[rows, :].astype(F32)).astype(BF)
        for t in range(2):
            lanes = slice(t * width, (t + 1) * width)
            mixed = mm(gated_ref[rows, lanes], ws_ref[0]) + mm(diffused[:, lanes], wn_ref[0])
            out_ref[rows, lanes] = (x_ref[rows, lanes].astype(F32) + mixed).astype(BF)

    by_blocks(x_ref.shape[0], body)


def mix(*arrays):
    return whole_call(
        mix_kernel, [(arrays[0].shape, BF)], [(array, VMEM_WHOLE) for array in arrays], flops=2 * 512 * 256 * 256
    )[0]


def layer_back_kernel(
    layer, dil_ref, x_ref, prior_ref, gz_ref, p_ref, f_ref, b_ref, wp_ref, wc_ref, ws_ref, wn_ref, *refs
):
    if layer:
        gx_ref, back_ref, gw_ref = refs
    else:
        upper_ref, gx_ref, back_ref, sent_ref, gw_ref = refs
    width = ws_ref.shape[1]
    near = dil_ref[layer] == 1
    wp, wc, ws, wn = wp_ref.at[layer], wc_ref.at[layer], ws_ref.at[layer], wn_ref.at[layer]
    gw_ref[...] = jnp.zeros_like(gw_ref)

    def body(rows):
        prevs = previous_days(near, x_ref[rows, :], prior_ref[rows, :])
        backs = []
        for t in range(2):
            lanes = slice(t * width, (t + 1) * width)
            x, prev = x_ref[rows, lanes], prevs[t]
            pre = mm(prev, wp[...]) + mm(x, wc[...])
            th = jnp.tanh(pre[:, :width])
            sg = jax.nn.sigmoid(pre[:, width:])
            gated = (th * sg).astype(BF)
            gz = gz_ref[rows, lanes]
            gzb = gz.astype(BF)
            spread = p_ref[lanes, rows] + f_ref[lanes, rows].astype(F32) + b_ref[lanes, rows].astype(F32)
            spread = jnp.transpose(spread).astype(BF)
            ggated = mm(gzb, ws[...], 1, 1) + mm(spread, wn[...], 1, 1)
            gpre = jnp.concatenate(
                [ggated * sg * (1.0 - th * th), ggated * th * sg * (1.0 - sg)], axis=1
            ).astype(BF)
            gw_ref[0:128, :] += mm(gated, gzb, 0, 0)
            gw_ref[128:256, :] += mm(gated, spread, 0, 0)
            gcur = mm(x, gpre, 0, 0)
            gw_ref[256:384, :] += gcur[:, :width]
            gw_ref[384:512, :] += gcur[:, width:]
            gprev = mm(prev, gpre, 0, 0)
            gw_ref[512:640, :] += gprev[:, :width]
            gw_ref[640:768, :] += gprev[:, width:]
            back = mm(gpre, wp[...], 1, 1)
            backs.append(back)
            back_ref[rows, lanes] = back.astype(BF)
            gx_ref[rows, lanes] = gz.astype(F32) + mm(gpre, wc[...], 1, 1)
        gx_ref[rows, :width] += jnp.where(near, backs[1], jnp.zeros_like(backs[1]))

    by_blocks(x_ref.shape[0], body)
    if not layer:
        for k in range(8):
            sent_ref[k] = gw_ref[96 * k : 96 * (k + 1), :].astype(BF)
            sent_ref[8 + k] = upper_ref[96 * k : 96 * (k + 1), :].astype(BF)


def layer_back(layer, dil, arrays, upper=None):
    shape = arrays[0].shape
    outs = [(shape, F32), (shape, BF), ((768, 128), F32)]
    if not layer:
        outs[2] = ((TMS, 96, 128), BF)
        arrays = arrays + [upper]
    return whole_call(
        lambda *refs: layer_back_kernel(layer, *refs),
        outs,
        [(dil, SMEM_WHOLE)] + [(array, VMEM_WHOLE) for array in arrays],
        flops=2 * 512 * 256 * 2048,
        bytes_accessed=4 << 20,
        scratch=[] if layer else [pltpu.VMEM((768, 128), F32)],
    )


def joined(near, gx, later):
    (gx_first, gx_second), (first, second) = halves(gx), halves(later)
    first, second = first.astype(F32), second.astype(F32)
    shift_first = jnp.where(near, jnp.zeros_like(first), first)
    shift_second = jnp.where(near, first, second)
    return gx_first.astype(F32) + shift_first, gx_second.astype(F32) + shift_second


def join_kernel(dil_ref, gx_ref, later_ref, gx_pair_ref, later_pair_ref, gz_ref, turned_ref, turned_pair_ref):
    near = dil_ref[1] == 1
    width = gx_ref.shape[1] // 2
    days = joined(near, gx_ref[...], later_ref[...])
    for t in range(2):
        lanes = slice(t * width, (t + 1) * width)
        gz_ref[:, lanes] = days[t]
        turned_ref[lanes, :] = jnp.transpose(days[t]).astype(BF)
    days = joined(near, gx_pair_ref[...], later_pair_ref[...])
    for t in range(2):
        turned_pair_ref[t * width : (t + 1) * width, :] = jnp.transpose(days[t]).astype(BF)


def join(dil, *arrays):
    rows, columns = arrays[0].shape
    return whole_call(
        join_kernel,
        [((rows, columns), F32), ((columns, rows), BF), ((columns, rows), BF)],
        [(dil, SMEM_WHOLE)] + [(array, VMEM_WHOLE) for array in arrays],
    )


def ring_step(ahead, aback):
    f, b = along_z(ahead, 1), along_z(aback, -1)
    return lax.optimization_barrier((f, b))


def ring_sum(send, parts):
    half = send.shape[0] // 2
    f, b = ring_step(send[:half], send[half:])
    ahead = jnp.concatenate([parts[0, :half] + f.astype(F32), parts[0, half:]], axis=0).astype(BF)
    aback = jnp.concatenate([parts[1, :half], parts[1, half:] + b.astype(F32)], axis=0).astype(BF)
    for s in (2, 4):
        f, b = ring_step(ahead, aback)
        ahead = (parts[s] + f.astype(F32)).astype(BF)
        aback = (parts[s + 1] + b.astype(F32)).astype(BF)
    return ring_step(ahead, aback)


def exchanged(chunks, axis):
    return lax.all_to_all(chunks, axis, 0, 0).astype(F32)


def sum_everywhere(chunks):
    mine = jnp.sum(exchanged(chunks, "tm"), axis=0).astype(BF)
    mine = jnp.sum(exchanged(jnp.broadcast_to(mine, (FIRMS,) + mine.shape), "firm"), axis=0).astype(BF)
    return exchanged(jnp.broadcast_to(mine, chunks.shape), "tm")


def from_pair_later(array):
    pairs = [((i ^ NZ) * TMS + t, i * TMS + t - 1) for i in range(FIRMS) for t in range(1, TMS)]
    return lax.ppermute(array, ("firm", "tm"), pairs)


def both_layers(features, cotangent, tiles, mask, w_prev, w_cur, w_self, w_nbr, dilations):
    rows, days, width = features.shape
    firm, tm = lax.axis_index("firm"), lax.axis_index("tm")
    pos = (firm * TMS + tm).astype(jnp.int32).reshape(1)
    weights = [w_prev, w_cur, w_self, w_nbr]

    piece = lend(pos, mask, tiles)
    state = features.reshape(rows, days * width)
    cot = cotangent.reshape(rows, days * width)
    lent = firm_xor(piece, NZ)
    prior = along_tm(behind(state, piece), 1)
    gated = gate(dilations, state, prior, w_prev, w_cur)

    half = width
    first = behind(lent, gated)
    before, after = along_x(first, 1), along_x(first, -1)
    other_first = tm_xor(first, 1)
    f1, b1 = along_z(gated, 1), along_z(gated, -1)
    pos_then = behind(pos, gated)
    own, cot_turned = prepare(pos_then, mask, tiles, cot)
    cot_pair = firm_xor(cot_turned, NZ)
    before, after, own, f1, b1 = lax.optimization_barrier((before, after, own, f1, b1))
    far = [along_x(before[:256], 1), along_x(after[256:], -1)]
    f2, b2 = along_z(f1, 1), along_z(b1, -1)
    sides = jnp.concatenate([after, before], axis=0)
    other_sides = tm_xor(sides, 1)
    f2, b2, cot_pair, far[0], far[1] = lax.optimization_barrier((f2, b2, cot_pair, far[0], far[1]))
    other_far = tm_xor(jnp.concatenate(far, axis=0), 1)
    f3, b3 = along_z(f2, 1), along_z(b2, -1)
    peer = gather_pieces(pos, [first, sides] + far + [other_first, other_sides, other_far])
    send, parts, last = spread_backward(pos, own, peer, cot_turned, cot_pair)
    f3, b3 = lax.optimization_barrier((f3, b3))
    f4, b4 = along_z(f3[:, :half], 1), along_z(b3[:, half:], -1)
    f4, b4 = lax.optimization_barrier((f4, b4))
    pieces = [gated, b1, b2, b3, f4, b4, f3, f2, f1]

    pos_then = behind(pos, send)
    mixed, other = spread_forward(pos_then, own, peer, pieces)
    next_state = mix(state, gated, mixed, firm_xor(other, NZ), w_self, w_nbr)
    next_prior = along_tm(next_state, 1)
    f, b = ring_sum(send, parts)
    gx, back, upper = layer_back(1, dilations, [next_state, next_prior, cot, last, f, b] + weights)

    gx_pair = firm_xor(gx.astype(BF), NZ)
    gz, gz_turned, gz_pair = join(dilations, gx, along_tm(back, -1), gx_pair, from_pair_later(back))
    send, parts, last = spread_backward(pos, own, peer, gz_turned, gz_pair)
    f, b = ring_sum(send, parts)
    gx, back, sent = layer_back(0, dilations, [state, prior, gz, last, f, b] + weights, upper)
    grad = jnp.stack(joined(dilations[0] == 1, gx, along_tm(back, -1)), axis=1)

    factor = 1.0 / jnp.sqrt(jnp.float32(rows * FIRMS * days * TMS))
    sums = sum_everywhere(sent).reshape(L, 768, width) * factor
    g_self, g_nbr = sums[:, 0:128], sums[:, 128:256]
    g_cur = jnp.concatenate([sums[:, 256:384], sums[:, 384:512]], axis=2)
    g_prev = jnp.concatenate([sums[:, 512:640], sums[:, 640:768]], axis=2)
    return grad, g_prev, g_cur, g_self, g_nbr


def solution(mesh):
    in_specs = (
        P("firm", "tm", None),
        P("firm", "tm", None),
        P("firm", None, None, None),
        P("firm", None),
        P(),
        P(),
        P(),
        P(),
        P(),
    )
    out_specs = (P("firm", "tm", None), P(), P(), P(), P())
    return jax.shard_map(both_layers, mesh=mesh, in_specs=in_specs, out_specs=out_specs, check_vma=False)
```

```python
import jax
import jax.numpy as jnp
from jax import lax
from jax.experimental import pallas as pl
from jax.experimental.pallas import tpu as pltpu
from jax.sharding import PartitionSpec as P


L = 2
NZ = 8
BF = jnp.bfloat16
F32 = jnp.float32

FIRMS = 16
TMS = 16
ANY = pl.BlockSpec(memory_space=pltpu.HBM)


def along_z(array, by):
    pairs = [(y * NZ + z, y * NZ + (z + by) % NZ) for y in range(2) for z in range(NZ)]
    return lax.ppermute(array, "firm", pairs)


def firm_xor(array, k):
    return lax.ppermute(array, "firm", [(i, i ^ k) for i in range(FIRMS)])


def tm_xor(array, k):
    return lax.ppermute(array, "tm", [(i, i ^ k) for i in range(TMS)])


def along_x(array, by):
    pairs = [(i, ((i // 4 + by) % 4) * 4 + i % 4) for i in range(TMS)]
    return lax.ppermute(array, "tm", pairs)


def along_tm(array, by):
    pairs = [(i, i + by) for i in range(TMS) if 0 <= i + by < TMS]
    return lax.ppermute(array, "tm", pairs)


def mm(a, b, ca=1, cb=0):
    return lax.dot_general(a, b, (((ca,), (cb,)), ((), ())), preferred_element_type=F32)


VMEM_WHOLE = pl.BlockSpec(memory_space=pltpu.VMEM)
SMEM_WHOLE = pl.BlockSpec(memory_space=pltpu.SMEM)


def whole_call(kernel, outs, ins, flops=0, bytes_accessed=1 << 20, scratch=(), grant=16 << 20):
    return pl.pallas_call(
        kernel,
        in_specs=[spec for _, spec in ins],
        out_specs=[VMEM_WHOLE for _ in outs],
        out_shape=[jax.ShapeDtypeStruct(shape, dtype) for shape, dtype in outs],
        scratch_shapes=list(scratch),
        cost_estimate=cost(flops, bytes_accessed),
        compiler_params=pltpu.CompilerParams(vmem_limit_bytes=grant),
    )(*[array for array, _ in ins])


def behind(array, *earlier):
    return lax.optimization_barrier((array,) + earlier)[0]


def cost(flops, bytes_accessed):
    return pl.CostEstimate(flops=flops, bytes_accessed=bytes_accessed, transcendentals=0)


def seat(pos):
    return pos // 128, (pos // 16) % 8, (pos // 4) % 4, pos % 2


def fetch(mask_ref, tiles_ref, target, sems, slot, block_column):
    copies = []
    for i in range(4):
        for j in range(4):
            copies.append(
                pltpu.make_async_copy(
                    tiles_ref.at[i, block_column * 4 + j],
                    target.at[i * 128 : (i + 1) * 128, j * 128 : (j + 1) * 128],
                    sems.at[slot, i * 4 + j],
                )
            )

    def finish():
        for copy in copies:
            copy.wait()
        for i in range(4):
            for j in range(4):

                @pl.when(mask_ref[i, block_column * 4 + j] == 0)
                def _():
                    target[i * 128 : (i + 1) * 128, j * 128 : (j + 1) * 128] = jnp.zeros((128, 128), BF)

    return copies, finish


def lend_kernel(pos_ref, mask_ref, tiles_ref, out_ref, sems):
    y, _, x, core = seat(pos_ref[0])
    copies, finish = fetch(mask_ref, tiles_ref, out_ref, sems, 0, (1 - y) * NZ + x * 2 + core)
    for copy in copies:
        copy.start()
    finish()


def lend(pos, mask, tiles):
    return whole_call(
        lend_kernel,
        [((512, 512), BF)],
        [(pos, SMEM_WHOLE), (mask, SMEM_WHOLE), (tiles, ANY)],
        scratch=[pltpu.SemaphoreType.DMA((1, 16))],
        grant=49 << 20,
    )[0]


def prepare_kernel(pos_ref, mask_ref, cot_ref, tiles_ref, out_ref, turned_ref, sems):
    width = cot_ref.shape[1] // 2
    base = seat(pos_ref[0])[0] * NZ

    def start(q, carry):
        for copy in fetch(mask_ref, tiles_ref, out_ref.at[q], sems, q, base + q)[0]:
            copy.start()
        return carry

    def finish(q, carry):
        fetch(mask_ref, tiles_ref, out_ref.at[q], sems, q, base + q)[1]()
        return carry

    lax.fori_loop(0, NZ, start, 0)
    for t in range(2):
        lanes = slice(t * width, (t + 1) * width)
        turned_ref[lanes, :] = jnp.transpose(cot_ref[:, lanes].astype(F32)).astype(BF)
    lax.fori_loop(0, NZ, finish, 0)


def prepare(pos, mask, tiles, cot):
    rows, columns = cot.shape
    return whole_call(
        prepare_kernel,
        [((NZ, 512, 512), BF), ((columns, rows), BF)],
        [(pos, SMEM_WHOLE), (mask, SMEM_WHOLE), (cot, VMEM_WHOLE), (tiles, ANY)],
        bytes_accessed=9 << 20,
        scratch=[pltpu.SemaphoreType.DMA((NZ, 16))],
        grant=49 << 20,
    )


def previous_days(near, x, prior):
    width = x.shape[1] // 2
    first = jnp.where(near, prior[:, width:], prior[:, :width])
    second = jnp.where(near, x[:, :width], prior[:, width:])
    return first, second


def halves(array):
    width = array.shape[1] // 2
    return array[:, :width], array[:, width:]


BLOCK = 256


def by_blocks(rows, body):
    def step(s, carry):
        body(pl.ds(pl.multiple_of(s * BLOCK, BLOCK), BLOCK))
        return carry

    lax.fori_loop(0, rows // BLOCK, step, 0)


def gate_kernel(dil_ref, x_ref, prior_ref, wp_ref, wc_ref, gated_ref):
    width = wp_ref.shape[1]
    near = dil_ref[0] == 1

    def body(rows):
        x = x_ref[rows, :]
        prevs = previous_days(near, x, prior_ref[rows, :])
        for t in range(2):
            lanes = slice(t * width, (t + 1) * width)
            pre = mm(prevs[t], wp_ref[0]) + mm(x[:, lanes], wc_ref[0])
            gated_ref[rows, lanes] = (jnp.tanh(pre[:, :width]) * jax.nn.sigmoid(pre[:, width:])).astype(BF)

    by_blocks(x_ref.shape[0], body)


def gate(dil, x, prior, wp, wc):
    return whole_call(
        gate_kernel,
        [(x.shape, BF)],
        [(dil, SMEM_WHOLE), (x, VMEM_WHOLE), (prior, VMEM_WHOLE), (wp, VMEM_WHOLE), (wc, VMEM_WHOLE)],
        flops=2 * 512 * 256 * 512,
    )[0]


def gather_kernel(pos_ref, first_ref, sides_ref, far0_ref, far1_ref, other_ref, other_sides_ref, other_far_ref, out_ref):
    _, _, x, core = seat(pos_ref[0])

    def column(step, sibling):
        return ((x + step) % 4) * 2 + (core if not sibling else 1 - core)

    out_ref[column(0, False)] = first_ref[...]
    out_ref[column(1, False)] = sides_ref[:512]
    out_ref[column(3, False)] = sides_ref[512:]
    out_ref[column(2, False), :256] = far0_ref[...]
    out_ref[column(2, False), 256:] = far1_ref[...]
    out_ref[column(0, True)] = other_ref[...]
    out_ref[column(1, True)] = other_sides_ref[:512]
    out_ref[column(3, True)] = other_sides_ref[512:]
    out_ref[column(2, True)] = other_far_ref[...]


def gather_pieces(pos, pieces):
    return whole_call(
        gather_kernel,
        [((NZ, 512, 512), BF)],
        [(pos, SMEM_WHOLE)] + [(piece, VMEM_WHOLE) for piece in pieces],
        bytes_accessed=8 << 20,
    )[0]


def spread_rows(pos_ref, own_ref, peer_ref, *refs):
    pieces, (out_own_ref, out_peer_ref, acc_ref, gathered) = refs[:9], refs[9:]
    z = seat(pos_ref[0])[1]
    for slot, ref in zip((0, 1, 2, 3, None, None, 5, 6, 7), pieces):
        if slot is not None:
            gathered[slot] = ref[...]
    gathered[4, :, :128] = pieces[4][...]
    gathered[4, :, 128:] = pieces[5][...]
    out_own_ref[...] = jnp.zeros_like(out_own_ref)
    acc_ref[...] = jnp.zeros_like(acc_ref)

    def step(q, carry):
        piece = gathered[(q - z + NZ) % NZ]
        out_own_ref[...] += mm(own_ref[q], piece)
        acc_ref[...] += mm(peer_ref[q], piece)
        return carry

    lax.fori_loop(0, NZ, step, 0)
    out_peer_ref[...] = acc_ref[...].astype(BF)


def spread_forward(pos, own, peer, pieces):
    shape = pieces[0].shape
    return whole_call(
        spread_rows,
        [(shape, F32), (shape, BF)],
        [(pos, SMEM_WHOLE), (own, VMEM_WHOLE), (peer, VMEM_WHOLE)] + [(piece, VMEM_WHOLE) for piece in pieces],
        flops=2 * 1024 * 4096 * 256,
        scratch=[pltpu.VMEM(shape, F32), pltpu.VMEM((NZ,) + shape, BF)],
    )


def ring_column(s, z):
    return (z + jnp.where(s % 2 == 1, (7 - s) // 2, s // 2 - 4) + NZ) % NZ


def spread_first(pos_ref, own_ref, peer_ref, mine_ref, theirs_ref, first_ref):
    q = ring_column(0, seat(pos_ref[0])[1])
    first_ref[...] = (mm(mine_ref[...], own_ref[q]) + mm(theirs_ref[...], peer_ref[q])).astype(BF)


def spread_columns(pos_ref, own_ref, peer_ref, mine_ref, theirs_ref, out_ref, last_ref):
    z = seat(pos_ref[0])[1]

    def step(s, carry):
        q = ring_column(s, z)
        total = mm(mine_ref[...], own_ref[q]) + mm(theirs_ref[...], peer_ref[q])

        @pl.when(s < NZ - 1)
        def _():
            out_ref[jnp.minimum(s - 1, NZ - 3)] = total

        @pl.when(s == NZ - 1)
        def _():
            last_ref[...] = total

        return carry

    lax.fori_loop(1, NZ, step, 0)


def spread_backward(pos, own, peer, mine, theirs):
    shape = mine.shape
    ins = [(pos, SMEM_WHOLE), (own, VMEM_WHOLE), (peer, VMEM_WHOLE), (mine, VMEM_WHOLE), (theirs, VMEM_WHOLE)]
    send = whole_call(spread_first, [(shape, BF)], ins, flops=2 * 1024 * 512 * 256)[0]
    ins[0] = (behind(pos, send), SMEM_WHOLE)
    outs = [((NZ - 2,) + shape, F32), (shape, F32)]
    parts, last = whole_call(spread_columns, outs, ins, flops=2 * 1024 * 3584 * 256)
    return send, parts, last


def mix_kernel(x_ref, gated_ref, own_ref, other_ref, ws_ref, wn_ref, out_ref):
    width = ws_ref.shape[1]

    def body(rows):
        diffused = (own_ref[rows, :] + other_ref[rows, :].astype(F32)).astype(BF)
        for t in range(2):
            lanes = slice(t * width, (t + 1) * width)
            mixed = mm(gated_ref[rows, lanes], ws_ref[0]) + mm(diffused[:, lanes], wn_ref[0])
            out_ref[rows, lanes] = (x_ref[rows, lanes].astype(F32) + mixed).astype(BF)

    by_blocks(x_ref.shape[0], body)


def mix(*arrays):
    return whole_call(
        mix_kernel, [(arrays[0].shape, BF)], [(array, VMEM_WHOLE) for array in arrays], flops=2 * 512 * 256 * 256
    )[0]


def layer_back_kernel(
    layer, dil_ref, x_ref, prior_ref, gz_ref, p_ref, f_ref, b_ref, wp_ref, wc_ref, ws_ref, wn_ref, *refs
):
    if layer:
        gx_ref, back_ref, gw_ref = refs
    else:
        upper_ref, gx_ref, back_ref, sent_ref, gw_ref = refs
    width = ws_ref.shape[1]
    near = dil_ref[layer] == 1
    wp, wc, ws, wn = wp_ref.at[layer], wc_ref.at[layer], ws_ref.at[layer], wn_ref.at[layer]
    gw_ref[...] = jnp.zeros_like(gw_ref)

    def body(rows):
        prevs = previous_days(near, x_ref[rows, :], prior_ref[rows, :])
        backs = []
        for t in range(2):
            lanes = slice(t * width, (t + 1) * width)
            x, prev = x_ref[rows, lanes], prevs[t]
            pre = mm(prev, wp[...]) + mm(x, wc[...])
            th = jnp.tanh(pre[:, :width])
            sg = jax.nn.sigmoid(pre[:, width:])
            gated = (th * sg).astype(BF)
            gz = gz_ref[rows, lanes]
            gzb = gz.astype(BF)
            spread = p_ref[lanes, rows] + f_ref[lanes, rows].astype(F32) + b_ref[lanes, rows].astype(F32)
            spread = jnp.transpose(spread).astype(BF)
            ggated = mm(gzb, ws[...], 1, 1) + mm(spread, wn[...], 1, 1)
            gpre = jnp.concatenate(
                [ggated * sg * (1.0 - th * th), ggated * th * sg * (1.0 - sg)], axis=1
            ).astype(BF)
            gw_ref[0:128, :] += mm(gated, gzb, 0, 0)
            gw_ref[128:256, :] += mm(gated, spread, 0, 0)
            gcur = mm(x, gpre, 0, 0)
            gw_ref[256:384, :] += gcur[:, :width]
            gw_ref[384:512, :] += gcur[:, width:]
            gprev = mm(prev, gpre, 0, 0)
            gw_ref[512:640, :] += gprev[:, :width]
            gw_ref[640:768, :] += gprev[:, width:]
            back = mm(gpre, wp[...], 1, 1)
            backs.append(back)
            back_ref[rows, lanes] = back.astype(BF)
            gx_ref[rows, lanes] = gz.astype(F32) + mm(gpre, wc[...], 1, 1)
        gx_ref[rows, :width] += jnp.where(near, backs[1], jnp.zeros_like(backs[1]))

    by_blocks(x_ref.shape[0], body)
    if not layer:
        for k in range(8):
            sent_ref[k] = gw_ref[96 * k : 96 * (k + 1), :].astype(BF)
            sent_ref[8 + k] = upper_ref[96 * k : 96 * (k + 1), :].astype(BF)


def layer_back(layer, dil, arrays, upper=None):
    shape = arrays[0].shape
    outs = [(shape, F32), (shape, BF), ((768, 128), F32)]
    if not layer:
        outs[2] = ((TMS, 96, 128), BF)
        arrays = arrays + [upper]
    return whole_call(
        lambda *refs: layer_back_kernel(layer, *refs),
        outs,
        [(dil, SMEM_WHOLE)] + [(array, VMEM_WHOLE) for array in arrays],
        flops=2 * 512 * 256 * 2048,
        bytes_accessed=4 << 20,
        scratch=[] if layer else [pltpu.VMEM((768, 128), F32)],
    )


def joined(near, gx, later):
    (gx_first, gx_second), (first, second) = halves(gx), halves(later)
    first, second = first.astype(F32), second.astype(F32)
    shift_first = jnp.where(near, jnp.zeros_like(first), first)
    shift_second = jnp.where(near, first, second)
    return gx_first.astype(F32) + shift_first, gx_second.astype(F32) + shift_second


def join_kernel(dil_ref, gx_ref, later_ref, gx_pair_ref, later_pair_ref, gz_ref, turned_ref, turned_pair_ref):
    near = dil_ref[1] == 1
    width = gx_ref.shape[1] // 2
    days = joined(near, gx_ref[...], later_ref[...])
    for t in range(2):
        lanes = slice(t * width, (t + 1) * width)
        gz_ref[:, lanes] = days[t]
        turned_ref[lanes, :] = jnp.transpose(days[t]).astype(BF)
    days = joined(near, gx_pair_ref[...], later_pair_ref[...])
    for t in range(2):
        turned_pair_ref[t * width : (t + 1) * width, :] = jnp.transpose(days[t]).astype(BF)


def join(dil, *arrays):
    rows, columns = arrays[0].shape
    return whole_call(
        join_kernel,
        [((rows, columns), F32), ((columns, rows), BF), ((columns, rows), BF)],
        [(dil, SMEM_WHOLE)] + [(array, VMEM_WHOLE) for array in arrays],
    )


def ring_step(ahead, aback):
    f, b = along_z(ahead, 1), along_z(aback, -1)
    return lax.optimization_barrier((f, b))


def ring_sum(send, parts):
    half = send.shape[0] // 2
    f, b = ring_step(send[:half], send[half:])
    ahead = jnp.concatenate([parts[0, :half] + f.astype(F32), parts[0, half:]], axis=0).astype(BF)
    aback = jnp.concatenate([parts[1, :half], parts[1, half:] + b.astype(F32)], axis=0).astype(BF)
    for s in (2, 4):
        f, b = ring_step(ahead, aback)
        ahead = (parts[s] + f.astype(F32)).astype(BF)
        aback = (parts[s + 1] + b.astype(F32)).astype(BF)
    return ring_step(ahead, aback)


def exchanged(chunks, axis):
    return lax.all_to_all(chunks, axis, 0, 0).astype(F32)


def sum_everywhere(chunks):
    mine = jnp.sum(exchanged(chunks, "tm"), axis=0).astype(BF)
    mine = jnp.sum(exchanged(jnp.broadcast_to(mine, (FIRMS,) + mine.shape), "firm"), axis=0).astype(BF)
    return lax.all_to_all(jnp.broadcast_to(mine, chunks.shape), "tm", 0, 0)


def unpack_kernel(factor, sums_ref, prev_ref, cur_ref, self_ref, nbr_ref):
    for layer in range(L):

        def rows(k):
            return sums_ref[layer, 128 * k : 128 * (k + 1), :].astype(F32) * factor

        self_ref[layer] = rows(0)
        nbr_ref[layer] = rows(1)
        for t in range(2):
            cur_ref[layer, :, 128 * t : 128 * (t + 1)] = rows(2 + t)
            prev_ref[layer, :, 128 * t : 128 * (t + 1)] = rows(4 + t)


def unpack(sums, factor):
    wide, narrow = (L, 128, 256), (L, 128, 128)
    return whole_call(
        lambda *refs: unpack_kernel(factor, *refs),
        [(wide, F32), (wide, F32), (narrow, F32), (narrow, F32)],
        [(sums, VMEM_WHOLE)],
    )


def from_pair_later(array):
    pairs = [((i ^ NZ) * TMS + t, i * TMS + t - 1) for i in range(FIRMS) for t in range(1, TMS)]
    return lax.ppermute(array, ("firm", "tm"), pairs)


def both_layers(features, cotangent, tiles, mask, w_prev, w_cur, w_self, w_nbr, dilations):
    rows, days, width = features.shape
    firm, tm = lax.axis_index("firm"), lax.axis_index("tm")
    pos = (firm * TMS + tm).astype(jnp.int32).reshape(1)
    weights = [w_prev, w_cur, w_self, w_nbr]

    piece = lend(pos, mask, tiles)
    state = features.reshape(rows, days * width)
    cot = cotangent.reshape(rows, days * width)
    lent = firm_xor(piece, NZ)
    prior = along_tm(behind(state, piece), 1)
    prior, first = lax.optimization_barrier((prior, lent))
    gated = gate(dilations, state, prior, w_prev, w_cur)

    half = width
    before, after = along_x(first, 1), along_x(first, -1)
    other_first = tm_xor(first, 1)
    f1, b1 = along_z(gated, 1), along_z(gated, -1)
    pos_then = behind(pos, gated)
    own, cot_turned = prepare(pos_then, mask, tiles, cot)
    cot_pair = firm_xor(cot_turned, NZ)
    before, after, own, f1, b1 = lax.optimization_barrier((before, after, own, f1, b1))
    far = [along_x(before[:256], 1), along_x(after[256:], -1)]
    f2, b2 = along_z(f1, 1), along_z(b1, -1)
    sides = jnp.concatenate([after, before], axis=0)
    other_sides = tm_xor(sides, 1)
    far = list(lax.optimization_barrier(tuple(far)))
    f2, b2 = lax.optimization_barrier((f2, b2))
    other_far = tm_xor(jnp.concatenate(far, axis=0), 1)
    f3, b3 = along_z(f2, 1), along_z(b2, -1)
    peer = gather_pieces(pos, [first, sides] + far + [other_first, other_sides, other_far])
    send, parts, last = spread_backward(pos, own, peer, cot_turned, cot_pair)
    f3, b3 = lax.optimization_barrier((f3, b3))
    f4, b4 = along_z(f3[:, :half], 1), along_z(b3[:, half:], -1)
    f4, b4 = lax.optimization_barrier((f4, b4))
    pieces = [gated, b1, b2, b3, f4, b4, f3, f2, f1]

    pos_then = behind(pos, send)
    mixed, other = spread_forward(pos_then, own, peer, pieces)
    next_state = mix(state, gated, mixed, firm_xor(other, NZ), w_self, w_nbr)
    next_prior = along_tm(next_state, 1)
    f, b = ring_sum(send, parts)
    gx, back, upper = layer_back(1, dilations, [next_state, next_prior, cot, last, f, b] + weights)

    gx_pair = firm_xor(gx.astype(BF), NZ)
    gz, gz_turned, gz_pair = join(dilations, gx, along_tm(back, -1), gx_pair, from_pair_later(back))
    send, parts, last = spread_backward(pos, own, peer, gz_turned, gz_pair)
    f, b = ring_sum(send, parts)
    gx, back, sent = layer_back(0, dilations, [state, prior, gz, last, f, b] + weights, upper)
    grad = jnp.stack(joined(dilations[0] == 1, gx, along_tm(back, -1)), axis=1)

    factor = (rows * FIRMS * days * TMS) ** -0.5
    return (grad,) + tuple(unpack(sum_everywhere(sent).reshape(L, 768, width), factor))


def solution(mesh):
    in_specs = (
        P("firm", "tm", None),
        P("firm", "tm", None),
        P("firm", None, None, None),
        P("firm", None),
        P(),
        P(),
        P(),
        P(),
        P(),
    )
    out_specs = (P("firm", "tm", None), P(), P(), P(), P())
    return jax.shard_map(both_layers, mesh=mesh, in_specs=in_specs, out_specs=out_specs, check_vma=False)
```

```python
import jax
import jax.numpy as jnp
from jax import lax
from jax.experimental import pallas as pl
from jax.experimental.pallas import tpu as pltpu
from jax.sharding import PartitionSpec as P


L = 2
NZ = 8
BF = jnp.bfloat16
F32 = jnp.float32

FIRMS = 16
TMS = 16
ANY = pl.BlockSpec(memory_space=pltpu.HBM)


def along_z(array, by):
    pairs = [(y * NZ + z, y * NZ + (z + by) % NZ) for y in range(2) for z in range(NZ)]
    return lax.ppermute(array, "firm", pairs)


def firm_xor(array, k):
    return lax.ppermute(array, "firm", [(i, i ^ k) for i in range(FIRMS)])


def tm_xor(array, k):
    return lax.ppermute(array, "tm", [(i, i ^ k) for i in range(TMS)])


def along_x(array, by):
    pairs = [(i, ((i // 4 + by) % 4) * 4 + i % 4) for i in range(TMS)]
    return lax.ppermute(array, "tm", pairs)


def along_tm(array, by):
    pairs = [(i, i + by) for i in range(TMS) if 0 <= i + by < TMS]
    return lax.ppermute(array, "tm", pairs)


def mm(a, b, ca=1, cb=0):
    return lax.dot_general(a, b, (((ca,), (cb,)), ((), ())), preferred_element_type=F32)


VMEM_WHOLE = pl.BlockSpec(memory_space=pltpu.VMEM)
SMEM_WHOLE = pl.BlockSpec(memory_space=pltpu.SMEM)


def whole_call(kernel, outs, ins, flops=0, bytes_accessed=1 << 20, scratch=(), grant=16 << 20):
    return pl.pallas_call(
        kernel,
        in_specs=[spec for _, spec in ins],
        out_specs=[VMEM_WHOLE for _ in outs],
        out_shape=[jax.ShapeDtypeStruct(shape, dtype) for shape, dtype in outs],
        scratch_shapes=list(scratch),
        cost_estimate=cost(flops, bytes_accessed),
        compiler_params=pltpu.CompilerParams(vmem_limit_bytes=grant),
    )(*[array for array, _ in ins])


def behind(array, *earlier):
    return lax.optimization_barrier((array,) + earlier)[0]


def cost(flops, bytes_accessed):
    return pl.CostEstimate(flops=flops, bytes_accessed=bytes_accessed, transcendentals=0)


def seat(pos):
    return pos // 128, (pos // 16) % 8, (pos // 4) % 4, pos % 2


def fetch(mask_ref, tiles_ref, target, sems, slot, block_column):
    copies = []
    for i in range(4):
        for j in range(4):
            copies.append(
                pltpu.make_async_copy(
                    tiles_ref.at[i, block_column * 4 + j],
                    target.at[i * 128 : (i + 1) * 128, j * 128 : (j + 1) * 128],
                    sems.at[slot, i * 4 + j],
                )
            )

    def finish():
        for copy in copies:
            copy.wait()
        for i in range(4):
            for j in range(4):

                @pl.when(mask_ref[i, block_column * 4 + j] == 0)
                def _():
                    target[i * 128 : (i + 1) * 128, j * 128 : (j + 1) * 128] = jnp.zeros((128, 128), BF)

    return copies, finish


def lend_kernel(pos_ref, mask_ref, tiles_ref, out_ref, sems):
    y, _, x, core = seat(pos_ref[0])
    copies, finish = fetch(mask_ref, tiles_ref, out_ref, sems, 0, (1 - y) * NZ + x * 2 + core)
    for copy in copies:
        copy.start()
    finish()


def lend(pos, mask, tiles):
    return whole_call(
        lend_kernel,
        [((512, 512), BF)],
        [(pos, SMEM_WHOLE), (mask, SMEM_WHOLE), (tiles, ANY)],
        scratch=[pltpu.SemaphoreType.DMA((1, 16))],
        grant=49 << 20,
    )[0]


def prepare_kernel(pos_ref, mask_ref, cot_ref, tiles_ref, out_ref, turned_ref, sems):
    width = cot_ref.shape[1] // 2
    base = seat(pos_ref[0])[0] * NZ

    def start(q, carry):
        for copy in fetch(mask_ref, tiles_ref, out_ref.at[q], sems, q, base + q)[0]:
            copy.start()
        return carry

    def finish(q, carry):
        fetch(mask_ref, tiles_ref, out_ref.at[q], sems, q, base + q)[1]()
        return carry

    lax.fori_loop(0, NZ, start, 0)
    for t in range(2):
        lanes = slice(t * width, (t + 1) * width)
        turned_ref[lanes, :] = jnp.transpose(cot_ref[:, lanes].astype(F32)).astype(BF)
    lax.fori_loop(0, NZ, finish, 0)


def prepare(pos, mask, tiles, cot):
    rows, columns = cot.shape
    return whole_call(
        prepare_kernel,
        [((NZ, 512, 512), BF), ((columns, rows), BF)],
        [(pos, SMEM_WHOLE), (mask, SMEM_WHOLE), (cot, VMEM_WHOLE), (tiles, ANY)],
        bytes_accessed=9 << 20,
        scratch=[pltpu.SemaphoreType.DMA((NZ, 16))],
        grant=49 << 20,
    )


def previous_days(near, x, prior):
    width = x.shape[1] // 2
    first = jnp.where(near, prior[:, width:], prior[:, :width])
    second = jnp.where(near, x[:, :width], prior[:, width:])
    return first, second


def halves(array):
    width = array.shape[1] // 2
    return array[:, :width], array[:, width:]


BLOCK = 256


def by_blocks(rows, body):
    def step(s, carry):
        body(pl.ds(pl.multiple_of(s * BLOCK, BLOCK), BLOCK))
        return carry

    lax.fori_loop(0, rows // BLOCK, step, 0)


def gate_kernel(dil_ref, x_ref, prior_ref, wp_ref, wc_ref, gated_ref):
    width = wp_ref.shape[1]
    near = dil_ref[0] == 1

    def body(rows):
        x = x_ref[rows, :]
        prevs = previous_days(near, x, prior_ref[rows, :])
        for t in range(2):
            lanes = slice(t * width, (t + 1) * width)
            pre = mm(prevs[t], wp_ref[0]) + mm(x[:, lanes], wc_ref[0])
            gated_ref[rows, lanes] = (jnp.tanh(pre[:, :width]) * jax.nn.sigmoid(pre[:, width:])).astype(BF)

    by_blocks(x_ref.shape[0], body)


def gate(dil, x, prior, wp, wc):
    return whole_call(
        gate_kernel,
        [(x.shape, BF)],
        [(dil, SMEM_WHOLE), (x, VMEM_WHOLE), (prior, VMEM_WHOLE), (wp, VMEM_WHOLE), (wc, VMEM_WHOLE)],
        flops=2 * 512 * 256 * 512,
    )[0]


def gather_kernel(pos_ref, first_ref, sides_ref, far0_ref, far1_ref, other_ref, other_sides_ref, other_far_ref, out_ref):
    _, _, x, core = seat(pos_ref[0])

    def column(step, sibling):
        return ((x + step) % 4) * 2 + (core if not sibling else 1 - core)

    out_ref[column(0, False)] = first_ref[...]
    out_ref[column(1, False)] = sides_ref[:512]
    out_ref[column(3, False)] = sides_ref[512:]
    out_ref[column(2, False), :256] = far0_ref[...]
    out_ref[column(2, False), 256:] = far1_ref[...]
    out_ref[column(0, True)] = other_ref[...]
    out_ref[column(1, True)] = other_sides_ref[:512]
    out_ref[column(3, True)] = other_sides_ref[512:]
    out_ref[column(2, True)] = other_far_ref[...]


def gather_pieces(pos, pieces):
    return whole_call(
        gather_kernel,
        [((NZ, 512, 512), BF)],
        [(pos, SMEM_WHOLE)] + [(piece, VMEM_WHOLE) for piece in pieces],
        bytes_accessed=8 << 20,
    )[0]


def spread_rows(pos_ref, own_ref, peer_ref, *refs):
    pieces, (out_own_ref, out_peer_ref, acc_ref, gathered) = refs[:9], refs[9:]
    z = seat(pos_ref[0])[1]
    for slot, ref in zip((0, 1, 2, 3, None, None, 5, 6, 7), pieces):
        if slot is not None:
            gathered[slot] = ref[...]
    gathered[4, :, :128] = pieces[4][...]
    gathered[4, :, 128:] = pieces[5][...]
    out_own_ref[...] = jnp.zeros_like(out_own_ref)
    acc_ref[...] = jnp.zeros_like(acc_ref)

    def step(q, carry):
        piece = gathered[(q - z + NZ) % NZ]
        out_own_ref[...] += mm(own_ref[q], piece)
        acc_ref[...] += mm(peer_ref[q], piece)
        return carry

    lax.fori_loop(0, NZ, step, 0)
    out_peer_ref[...] = acc_ref[...].astype(BF)


def spread_forward(pos, own, peer, pieces):
    shape = pieces[0].shape
    return whole_call(
        spread_rows,
        [(shape, F32), (shape, BF)],
        [(pos, SMEM_WHOLE), (own, VMEM_WHOLE), (peer, VMEM_WHOLE)] + [(piece, VMEM_WHOLE) for piece in pieces],
        flops=2 * 1024 * 4096 * 256,
        scratch=[pltpu.VMEM(shape, F32), pltpu.VMEM((NZ,) + shape, BF)],
    )


def ring_column(s, z):
    return (z + jnp.where(s % 2 == 1, (7 - s) // 2, s // 2 - 4) + NZ) % NZ


def spread_first(pos_ref, own_ref, peer_ref, mine_ref, theirs_ref, first_ref):
    q = ring_column(0, seat(pos_ref[0])[1])
    first_ref[...] = (mm(mine_ref[...], own_ref[q]) + mm(theirs_ref[...], peer_ref[q])).astype(BF)


def spread_columns(pos_ref, own_ref, peer_ref, mine_ref, theirs_ref, out_ref, last_ref):
    z = seat(pos_ref[0])[1]

    def step(s, carry):
        q = ring_column(s, z)
        total = mm(mine_ref[...], own_ref[q]) + mm(theirs_ref[...], peer_ref[q])

        @pl.when(s < NZ - 1)
        def _():
            out_ref[jnp.minimum(s - 1, NZ - 3)] = total

        @pl.when(s == NZ - 1)
        def _():
            last_ref[...] = total

        return carry

    lax.fori_loop(1, NZ, step, 0)


def spread_backward(pos, own, peer, mine, theirs):
    shape = mine.shape
    ins = [(pos, SMEM_WHOLE), (own, VMEM_WHOLE), (peer, VMEM_WHOLE), (mine, VMEM_WHOLE), (theirs, VMEM_WHOLE)]
    send = whole_call(spread_first, [(shape, BF)], ins, flops=2 * 1024 * 512 * 256)[0]
    ins[0] = (behind(pos, send), SMEM_WHOLE)
    outs = [((NZ - 2,) + shape, F32), (shape, F32)]
    parts, last = whole_call(spread_columns, outs, ins, flops=2 * 1024 * 3584 * 256)
    return send, parts, last


def mix_kernel(x_ref, gated_ref, own_ref, other_ref, ws_ref, wn_ref, out_ref):
    width = ws_ref.shape[1]

    def body(rows):
        diffused = (own_ref[rows, :] + other_ref[rows, :].astype(F32)).astype(BF)
        for t in range(2):
            lanes = slice(t * width, (t + 1) * width)
            mixed = mm(gated_ref[rows, lanes], ws_ref[0]) + mm(diffused[:, lanes], wn_ref[0])
            out_ref[rows, lanes] = (x_ref[rows, lanes].astype(F32) + mixed).astype(BF)

    by_blocks(x_ref.shape[0], body)


def mix(*arrays):
    return whole_call(
        mix_kernel, [(arrays[0].shape, BF)], [(array, VMEM_WHOLE) for array in arrays], flops=2 * 512 * 256 * 256
    )[0]


def layer_back_kernel(
    layer, dil_ref, x_ref, prior_ref, gz_ref, p_ref, f_ref, b_ref, wp_ref, wc_ref, ws_ref, wn_ref, *refs
):
    if layer:
        gx_ref, back_ref, gw_ref = refs
    else:
        upper_ref, gx_ref, back_ref, sent_ref, gw_ref = refs
    width = ws_ref.shape[1]
    near = dil_ref[layer] == 1
    wp, wc, ws, wn = wp_ref.at[layer], wc_ref.at[layer], ws_ref.at[layer], wn_ref.at[layer]
    gw_ref[...] = jnp.zeros_like(gw_ref)

    def body(rows):
        prevs = previous_days(near, x_ref[rows, :], prior_ref[rows, :])
        backs = []
        for t in range(2):
            lanes = slice(t * width, (t + 1) * width)
            x, prev = x_ref[rows, lanes], prevs[t]
            pre = mm(prev, wp[...]) + mm(x, wc[...])
            th = jnp.tanh(pre[:, :width])
            sg = jax.nn.sigmoid(pre[:, width:])
            gated = (th * sg).astype(BF)
            gz = gz_ref[rows, lanes]
            gzb = gz.astype(BF)
            spread = p_ref[lanes, rows] + f_ref[lanes, rows].astype(F32) + b_ref[lanes, rows].astype(F32)
            spread = jnp.transpose(spread).astype(BF)
            ggated = mm(gzb, ws[...], 1, 1) + mm(spread, wn[...], 1, 1)
            gpre = jnp.concatenate(
                [ggated * sg * (1.0 - th * th), ggated * th * sg * (1.0 - sg)], axis=1
            ).astype(BF)
            gw_ref[0:128, :] += mm(gated, gzb, 0, 0)
            gw_ref[128:256, :] += mm(gated, spread, 0, 0)
            gcur = mm(x, gpre, 0, 0)
            gw_ref[256:384, :] += gcur[:, :width]
            gw_ref[384:512, :] += gcur[:, width:]
            gprev = mm(prev, gpre, 0, 0)
            gw_ref[512:640, :] += gprev[:, :width]
            gw_ref[640:768, :] += gprev[:, width:]
            back = mm(gpre, wp[...], 1, 1)
            backs.append(back)
            back_ref[rows, lanes] = back.astype(BF)
            gx_ref[rows, lanes] = gz.astype(F32) + mm(gpre, wc[...], 1, 1)
        gx_ref[rows, :width] += jnp.where(near, backs[1], jnp.zeros_like(backs[1]))

    by_blocks(x_ref.shape[0], body)
    if not layer:
        for k in range(8):
            sent_ref[k] = gw_ref[96 * k : 96 * (k + 1), :].astype(BF)
            sent_ref[8 + k] = upper_ref[96 * k : 96 * (k + 1), :].astype(BF)


def layer_back(layer, dil, arrays, upper=None):
    shape = arrays[0].shape
    outs = [(shape, F32), (shape, BF), ((768, 128), F32)]
    if not layer:
        outs[2] = ((TMS, 96, 128), BF)
        arrays = arrays + [upper]
    return whole_call(
        lambda *refs: layer_back_kernel(layer, *refs),
        outs,
        [(dil, SMEM_WHOLE)] + [(array, VMEM_WHOLE) for array in arrays],
        flops=2 * 512 * 256 * 2048,
        bytes_accessed=4 << 20,
        scratch=[] if layer else [pltpu.VMEM((768, 128), F32)],
    )


def joined(near, gx, later):
    (gx_first, gx_second), (first, second) = halves(gx), halves(later)
    first, second = first.astype(F32), second.astype(F32)
    shift_first = jnp.where(near, jnp.zeros_like(first), first)
    shift_second = jnp.where(near, first, second)
    return gx_first.astype(F32) + shift_first, gx_second.astype(F32) + shift_second


def join_kernel(dil_ref, gx_ref, later_ref, gx_pair_ref, later_pair_ref, gz_ref, turned_ref, turned_pair_ref):
    near = dil_ref[1] == 1
    width = gx_ref.shape[1] // 2
    days = joined(near, gx_ref[...], later_ref[...])
    for t in range(2):
        lanes = slice(t * width, (t + 1) * width)
        gz_ref[:, lanes] = days[t]
        turned_ref[lanes, :] = jnp.transpose(days[t]).astype(BF)
    days = joined(near, gx_pair_ref[...], later_pair_ref[...])
    for t in range(2):
        turned_pair_ref[t * width : (t + 1) * width, :] = jnp.transpose(days[t]).astype(BF)


def join(dil, *arrays):
    rows, columns = arrays[0].shape
    return whole_call(
        join_kernel,
        [((rows, columns), F32), ((columns, rows), BF), ((columns, rows), BF)],
        [(dil, SMEM_WHOLE)] + [(array, VMEM_WHOLE) for array in arrays],
    )


def ring_step(ahead, aback):
    f, b = along_z(ahead, 1), along_z(aback, -1)
    return lax.optimization_barrier((f, b))


def ring_sum(send, parts):
    half = send.shape[0] // 2
    f, b = ring_step(send[:half], send[half:])
    ahead = jnp.concatenate([parts[0, :half] + f.astype(F32), parts[0, half:]], axis=0).astype(BF)
    aback = jnp.concatenate([parts[1, :half], parts[1, half:] + b.astype(F32)], axis=0).astype(BF)
    for s in (2, 4):
        f, b = ring_step(ahead, aback)
        ahead = (parts[s] + f.astype(F32)).astype(BF)
        aback = (parts[s + 1] + b.astype(F32)).astype(BF)
    return ring_step(ahead, aback)


def exchanged(chunks, axis):
    return lax.all_to_all(chunks, axis, 0, 0).astype(F32)


def sum_everywhere(chunks):
    mine = jnp.sum(exchanged(chunks, "tm"), axis=0).astype(BF)
    mine = jnp.sum(exchanged(jnp.broadcast_to(mine, (FIRMS,) + mine.shape), "firm"), axis=0).astype(BF)
    return lax.all_to_all(jnp.broadcast_to(mine, chunks.shape), "tm", 0, 0)


def unpack_kernel(factor, sums_ref, prev_ref, cur_ref, self_ref, nbr_ref):
    for layer in range(L):

        def rows(k):
            return sums_ref[layer, 128 * k : 128 * (k + 1), :].astype(F32) * factor

        self_ref[layer] = rows(0)
        nbr_ref[layer] = rows(1)
        for t in range(2):
            cur_ref[layer, :, 128 * t : 128 * (t + 1)] = rows(2 + t)
            prev_ref[layer, :, 128 * t : 128 * (t + 1)] = rows(4 + t)


def unpack(sums, factor):
    wide, narrow = (L, 128, 256), (L, 128, 128)
    return whole_call(
        lambda *refs: unpack_kernel(factor, *refs),
        [(wide, F32), (wide, F32), (narrow, F32), (narrow, F32)],
        [(sums, VMEM_WHOLE)],
    )


def from_pair_later(array):
    pairs = [((i ^ NZ) * TMS + t, i * TMS + t - 1) for i in range(FIRMS) for t in range(1, TMS)]
    return lax.ppermute(array, ("firm", "tm"), pairs)


def both_layers(features, cotangent, tiles, mask, w_prev, w_cur, w_self, w_nbr, dilations):
    rows, days, width = features.shape
    firm, tm = lax.axis_index("firm"), lax.axis_index("tm")
    pos = (firm * TMS + tm).astype(jnp.int32).reshape(1)
    weights = [w_prev, w_cur, w_self, w_nbr]

    state = features.reshape(rows, days * width)
    cot = cotangent.reshape(rows, days * width)
    prior = along_tm(state, 1)
    lent = firm_xor(lend(pos, mask, tiles), NZ)
    gated = gate(dilations, state, prior, w_prev, w_cur)

    half = width
    f1, b1 = along_z(gated, 1), along_z(gated, -1)
    pos_then = behind(pos, gated)
    own, cot_turned = prepare(pos_then, mask, tiles, cot)
    first = behind(lent, own)
    before, after = along_x(first, 1), along_x(first, -1)
    other_first = tm_xor(first, 1)
    f1, b1 = lax.optimization_barrier((f1, b1))
    f2, b2 = along_z(f1, 1), along_z(b1, -1)
    cot_pair = firm_xor(cot_turned, NZ)
    before, after = lax.optimization_barrier((before, after))
    far = [along_x(before[:256], 1), along_x(after[256:], -1)]
    sides = jnp.concatenate([after, before], axis=0)
    other_sides = tm_xor(sides, 1)
    f2, b2 = lax.optimization_barrier((f2, b2))
    f3, b3 = along_z(f2, 1), along_z(b2, -1)
    far = list(lax.optimization_barrier(tuple(far)))
    other_far = tm_xor(jnp.concatenate(far, axis=0), 1)
    f3, b3 = lax.optimization_barrier((f3, b3))
    f4, b4 = along_z(f3[:, :half], 1), along_z(b3[:, half:], -1)
    f4, b4 = lax.optimization_barrier((f4, b4))
    peer = gather_pieces(pos, [first, sides] + far + [other_first, other_sides, other_far])
    send, parts, last = spread_backward(pos, own, peer, cot_turned, cot_pair)
    pieces = [gated, b1, b2, b3, f4, b4, f3, f2, f1]

    pos_then = behind(pos, send)
    mixed, other = spread_forward(pos_then, own, peer, pieces)
    next_state = mix(state, gated, mixed, firm_xor(other, NZ), w_self, w_nbr)
    next_prior = along_tm(next_state, 1)
    f, b = ring_sum(send, parts)
    gx, back, upper = layer_back(1, dilations, [next_state, next_prior, cot, last, f, b] + weights)

    later = along_tm(back, -1)
    later_pair = from_pair_later(back)
    gx_pair = firm_xor(gx.astype(BF), NZ)
    gz, gz_turned, gz_pair = join(dilations, gx, later, gx_pair, later_pair)
    send, parts, last = spread_backward(pos, own, peer, gz_turned, gz_pair)
    f, b = ring_sum(send, parts)
    gx, back, sent = layer_back(0, dilations, [state, prior, gz, last, f, b] + weights, upper)
    grad = jnp.stack(joined(dilations[0] == 1, gx, along_tm(back, -1)), axis=1)

    factor = (rows * FIRMS * days * TMS) ** -0.5
    return (grad,) + tuple(unpack(sum_everywhere(sent).reshape(L, 768, width), factor))


def solution(mesh):
    in_specs = (
        P("firm", "tm", None),
        P("firm", "tm", None),
        P("firm", None, None, None),
        P("firm", None),
        P(),
        P(),
        P(),
        P(),
        P(),
    )
    out_specs = (P("firm", "tm", None), P(), P(), P(), P())
    return jax.shard_map(both_layers, mesh=mesh, in_specs=in_specs, out_specs=out_specs, check_vma=False)
```
